128 devices in a mesh: basis: 4 (over z), pair: 32 (over x, y, core).
Axes of the slice: x: 4, y: 4, z: 4, core: 2. Of those that a mesh axis runs over, the one named last changes fastest.
Arguments:
- half_ints: bfloat16 [64, 16384, 256], P('pair', 'basis'), may hold values from -6 to 6
- pno_coef: bfloat16 [4, 128, 16384, 128], P(None, 'pair', 'basis'), may hold values from -0.046875 to 0.046875
- pair_list: int32 [4, 128, 2], P(None, 'pair'), may hold values from 0 to 63, as said below
- fit_domain: int32 [64, 256], P('pair'), may hold values from 0 to 32767
- fit_factor: bfloat16 [32768, 256], P('pair'), may hold values from -0.375 to 0.375
- amplitudes: bfloat16 [512, 128, 128], P(('basis', 'pair')), may hold values from -3 to 3
- pno_energy: float32 [512, 128], P(('basis', 'pair')), may hold values from 0.3 to 3
- occ_energy: float32 [64], replicated, may hold values from -2 to -0.3
- partners: int32 [512, 8], P(('basis', 'pair')), may hold values from 0 to 511, as said below
- partner_mask: int32 [512, 8], P(('basis', 'pair')), may hold values from 0 to 1, as said below
- intersections: bfloat16 [512, 8, 128, 128], P(('basis', 'pair')), may hold values from -0.5 to 0.5
- coupling: float32 [512, 8], P(('basis', 'pair')), may hold values from -3 to 3
Outputs:
- residual: float32 [512, 128, 128], P(('basis', 'pair'))
- new_amplitudes: bfloat16 [512, 128, 128], P(('basis', 'pair'))
The draws below stay inside these ranges and needn't reach their ends.
Inputs may be any that keep to these rules, and one draw needn't show every extreme that they name: pair_list[b, h, 0] lies in (h // 4) * 2 to (h // 4 + 1) * 2 - 1. `partners`: every partner of pair b * 128 + h lies in b * 128 to (b + 1) * 128 - 1; among the 32 slots of the pairs of one device, at most 2 name pairs of one device, and exactly 2 do for some device. `partner_mask`: the valid slots of each pair come first, and the first slot is valid.
All inputs are finite; a program needn't handle non-finite values.
Results may differ from the reference program's by a relative error of at most 0.008.
Values may be sent and summed in bfloat16 or wider, within the bound.
A program may use at most 128 MiB of HBM per device.

```python
import math
import jax
import jax.numpy as jnp
from jax import lax

NBAS = 16384
NPNO = 128
NFIT = 256
NPART = 8
PAIR_DEV = 4
OCC_DEV = 2
GROUP = 128
PAIRS = 512
NOCC = 64
NAUX = 32768
CAP = 2
N_BASIS = 4
N_PAIR = 32


def draw_pair_list(key, part):
    first_key = jax.random.fold_in(key, 11)
    second_key = jax.random.fold_in(key, 12)
    position = jnp.broadcast_to(jnp.arange(GROUP, dtype=jnp.int32)[None, :], (N_BASIS, GROUP))
    offset = jax.random.randint(first_key, (N_BASIS, GROUP), 0, OCC_DEV)
    first_orbital = position // PAIR_DEV * OCC_DEV + offset
    second = jax.random.randint(second_key, (N_BASIS, GROUP), 0, NOCC)
    return jnp.stack([first_orbital, second], axis=2).astype(jnp.int32)


def device_partners(base_key, device):
    slot_count = PAIR_DEV * NPART
    block_index = device // N_PAIR
    main_key, rest_key, order_key, within_key = jax.random.split(jax.random.fold_in(base_key, device), 4)
    busiest = jax.random.randint(main_key, (), 0, N_PAIR)
    spread = jax.random.permutation(rest_key, (N_PAIR - 1) * CAP)
    others = (spread // CAP + busiest + 1) % N_PAIR
    chosen = jnp.concatenate([jnp.full((CAP,), busiest, jnp.int32), others[:slot_count - CAP].astype(jnp.int32)])
    shuffled = chosen[jax.random.permutation(order_key, slot_count)]
    within_block = jax.random.randint(within_key, (slot_count,), 0, PAIR_DEV)
    return block_index * GROUP + shuffled * PAIR_DEV + within_block


def draw_partners(key, part):
    devices = jnp.arange(N_BASIS * N_PAIR, dtype=jnp.int32)
    base_key = jax.random.fold_in(key, 21)
    partner_table = jax.vmap(lambda device: device_partners(base_key, device))(devices)
    return partner_table.reshape(PAIRS, NPART).astype(jnp.int32)


def draw_partner_mask(key, part):
    counts = jax.random.randint(jax.random.fold_in(key, 31), (PAIRS, 1), 1, NPART + 1)
    slot_index = jnp.arange(NPART, dtype=jnp.int32)[None, :]
    return (slot_index < counts).astype(jnp.int32)


def place_ends(array, stream_key, low, high):
    longest = array.shape.index(max(array.shape))
    spots = []
    for shift in (0, 1):
        where = [jax.random.randint(jax.random.fold_in(stream_key, axis), (), 0, length) for axis, length in enumerate(array.shape)]
        where[longest] = (where[longest] + shift) % array.shape[longest]
        spots.append(tuple(where))
    return array.at[spots[0]].set(low).at[spots[1]].set(high)


def levels(own_key, shape, shards, least, top_value):
    def one(dim, parts):
        heights = jax.random.uniform(jax.random.fold_in(jax.random.fold_in(own_key, 6), dim), (parts,), jnp.float32, least / len(shards), top_value / len(shards))
        return jnp.repeat(jnp.exp(heights), shape[dim] // parts).reshape((-1,) + (1,) * (len(shape) - dim - 1))

    level = one(*shards[0])
    for cut in shards[1:]:
        level = level * one(*cut)
    return level


def scatter_about(stream_key, shape, scale, most, cuts=(), kind=jnp.bfloat16):
    drawn = jax.random.normal(stream_key, shape, jnp.float32) * scale
    if len(cuts) > 0:
        drawn = levels(stream_key, shape, cuts, -0.22, 0.18) * drawn
    return jnp.clip(drawn, min=-most, max=most).astype(kind)


def setup_inputs(seed: int = 0) -> dict:
    splits = jax.random.split(jax.random.key(seed), 13)
    half_ints = scatter_about(splits[0], (NOCC, NBAS, NFIT), 1.0, 6.0, ((0, 32), (1, 4)))
    pno_coef = scatter_about(splits[1], (N_BASIS, GROUP, NBAS, NPNO), NBAS ** -0.5, 0.046875, ((1, 32), (2, 4)))
    pair_list = draw_pair_list(jax.random.fold_in(splits[12], 71), 0)
    fit_domain = place_ends(jax.random.randint(splits[3], (NOCC, NFIT), 0, NAUX), jax.random.fold_in(splits[3], 1), 0, NAUX - 1).astype(jnp.int32)
    fit_factor = scatter_about(splits[4], (NAUX, NFIT), NFIT ** -0.5, 0.375, ((0, 32),))
    amplitudes = scatter_about(splits[5], (PAIRS, NPNO, NPNO), 0.5, 3.0, ((0, 128),))
    pno_energy = jnp.clip(jnp.exp(math.log(3.0) - 2.3025851 * jax.random.uniform(splits[6], (PAIRS, NPNO), jnp.float32) ** levels(splits[6], (PAIRS, NPNO), ((0, 128),), -0.2, 0.2)), 0.3, 3.0)
    occ_energy = jnp.clip(jax.random.uniform(splits[7], (NOCC,), jnp.float32, -2.0, -0.3), -2.0, -0.3)
    partners = draw_partners(jax.random.fold_in(splits[12], 71), 0)
    partner_mask = draw_partner_mask(jax.random.fold_in(splits[12], 71), 0)
    intersections = scatter_about(splits[10], (PAIRS, NPART, NPNO, NPNO), NPNO ** -0.5, 0.5, ((0, 128),))
    coupling = scatter_about(splits[11], (PAIRS, NPART), 0.5, 3.0, ((0, 128),), jnp.float32)
    return dict(half_ints=half_ints, pno_coef=pno_coef, pair_list=pair_list, fit_domain=fit_domain, fit_factor=fit_factor, amplitudes=amplitudes, pno_energy=pno_energy, occ_energy=occ_energy, partners=partners, partner_mask=partner_mask, intersections=intersections, coupling=coupling)


def reference(half_ints, pno_coef, pair_list, fit_domain, fit_factor, amplitudes, pno_energy, occ_energy, partners, partner_mask, intersections, coupling):
    coef_all = pno_coef.reshape((PAIRS, NBAS, NPNO))
    list_all = pair_list.reshape((PAIRS, 2))

    def one_pair(index):
        orbital = list_all[index, 0]
        other_orbital = list_all[index, 1]
        factor = jnp.dot(half_ints[orbital].T, coef_all[index], preferred_element_type=jnp.float32).astype(jnp.bfloat16)
        domain_rows = fit_factor[fit_domain[orbital]]
        fitted = jnp.dot(domain_rows.T, factor, preferred_element_type=jnp.float32).astype(jnp.bfloat16)
        exchange = jnp.dot(fitted.T, fitted, preferred_element_type=jnp.float32) / NFIT
        picked = amplitudes[partners[index]]
        intersection_one = intersections[index].astype(jnp.float32)
        projected = jnp.einsum("sab,sbc->sac", intersection_one, picked.astype(jnp.float32)).astype(jnp.bfloat16)
        carried = jnp.einsum("sac,sdc->sad", projected.astype(jnp.float32), intersection_one)
        weights = partner_mask[index].astype(jnp.float32) * coupling[index]
        coupled = jnp.sum(weights[:, None, None] * carried, axis=0)
        occ_sum = occ_energy[orbital] + occ_energy[other_orbital]
        energy_one = pno_energy[index]
        denominator = (energy_one[:, None] + energy_one[None, :]) - occ_sum
        amps = amplitudes[index].astype(jnp.float32)
        residual = (exchange + denominator * amps) + coupled
        updated = (amps - residual / denominator).astype(jnp.bfloat16)
        return residual, updated

    residual, updated = lax.map(one_pair, jnp.arange(PAIRS, dtype=jnp.int32))
    return residual, updated
```

```python
import jax
import jax.numpy as jnp
from jax import lax
from jax.experimental import pallas as pl
from jax.experimental.pallas import tpu as pltpu
from jax.sharding import PartitionSpec as P

BF = jnp.bfloat16
F32 = jnp.float32
MESH = pl.DeviceIdType.MESH
COPIES = 55
VMEM_LIMIT = 60 * 1024 * 1024


def kernel(
    half_hbm, coef_hbm, list_hbm, dom_hbm, fit_hbm, amp_hbm, pen_hbm, occ_hbm,
    part_hbm, mask_hbm, inter_hbm, coup_hbm,
    sum_ref, den_ref,
    hbuf, ht, cb0, cb1, cb2, cb3,
    am, fb, ft, tb, fd, rb, rr, dt, pb, gr2, gr, own, inter, pen,
    list_s, occ_s, part_s, mask_s, coup_s,
    send_sem, recv_sem, h_sem, c_sem, in_sem,
):
    cbs = (cb0, cb1, cb2, cb3)
    z = lax.axis_index("basis")
    pair = lax.axis_index("pair")
    x, y, c = pair // 8, (pair // 2) % 4, pair % 2
    xp, xm, x2 = (x + 1) % 4, (x + 3) % 4, (x + 2) % 4
    yp, ym, y2 = (y + 1) % 4, (y + 3) % 4, (y + 2) % 4
    zp, zm, z2 = (z + 1) % 4, (z + 3) % 4, (z + 2) % 4

    def dev(zz, xx, yy, cc):
        return (zz, (xx * 4 + yy) * 2 + cc)

    to = {
        "xp": dev(z, xp, y, c), "xm": dev(z, xm, y, c),
        "yp": dev(z, x, yp, c), "ym": dev(z, x, ym, c), "y2": dev(z, x, y2, c),
        "zp": dev(zp, x, y, c), "zm": dev(zm, x, y, c), "z2": dev(z2, x, y, c),
        "o": dev(z, x, y, 1 - c),
    }
    started = []
    numbers = {}

    def rdma(name, src, dst, where):
        number = numbers.setdefault(name, len(numbers))
        return pltpu.make_async_remote_copy(
            src_ref=src, dst_ref=dst, send_sem=send_sem.at[number], recv_sem=recv_sem.at[number],
            device_id=to[where], device_id_type=MESH,
        )

    def same(name, ref, where):
        return rdma(name, ref, ref, where)

    every = pl.ds(0, 4)
    cp = {
        "a1p": same("a1p", am.at[x, y, c, pl.ds(0, 2)], "xp"),
        "a1m": same("a1m", am.at[x, y, c, pl.ds(0, 2)], "xm"),
        "a1rp": same("a1rp", am.at[xm, y, c, 0], "xp"),
        "a1rm": same("a1rm", am.at[xp, y, c, 1], "xm"),
        "b1p": same("b1p", am.at[x, y, c, pl.ds(2, 2)], "yp"),
        "b1m": same("b1m", am.at[x, y, c, pl.ds(2, 2)], "ym"),
        "b1rp": same("b1rp", am.at[x, ym, c, 2], "yp"),
        "b1rm": same("b1rm", am.at[x, yp, c, 3], "ym"),
        "a2p0": same("a2p0", am.at[every, y, c, 0], "yp"),
        "a2p1": same("a2p1", am.at[every, y, c, 1], "yp"),
        "a2m0": same("a2m0", am.at[every, y, c, 0], "ym"),
        "a2m1": same("a2m1", am.at[every, y, c, 1], "ym"),
        "a2rp": same("a2rp", am.at[every, ym, c, 0], "yp"),
        "a2rm": same("a2rm", am.at[every, yp, c, 1], "ym"),
        "b2p0": same("b2p0", am.at[x, every, c, 2], "xp"),
        "b2p1": same("b2p1", am.at[x, every, c, 3], "xp"),
        "b2m0": same("b2m0", am.at[x, every, c, 2], "xm"),
        "b2m1": same("b2m1", am.at[x, every, c, 3], "xm"),
        "b2rp": same("b2rp", am.at[xm, every, c, 2], "xp"),
        "b2rm": same("b2rm", am.at[xp, every, c, 3], "xm"),
        "fa1": same("fa1", am.at[every, y, c, pl.ds(0, 2)], "o"),
        "fb1": same("fb1", am.at[x, every, c, pl.ds(2, 2)], "o"),
        "fa2m": same("fa2m", am.at[every, ym, c, pl.ds(0, 2)], "o"),
        "fa2p": same("fa2p", am.at[every, yp, c, pl.ds(0, 2)], "o"),
        "fa20": same("fa20", am.at[every, y2, c, 0], "o"),
        "fa21": same("fa21", am.at[every, y2, c, 1], "o"),
        "fb2m": same("fb2m", am.at[xm, every, c, pl.ds(2, 2)], "o"),
        "fb2p": same("fb2p", am.at[xp, every, c, pl.ds(2, 2)], "o"),
        "fb20": same("fb20", am.at[x2, every, c, 2], "o"),
        "fb21": same("fb21", am.at[x2, every, c, 3], "o"),
        "t1p0": rdma("t1p0", tb.at[0, 0, pl.ds(0, 128)], tb.at[0, 1, pl.ds(0, 128)], "xp"),
        "t1p1": rdma("t1p1", tb.at[0, 0, pl.ds(128, 128)], tb.at[0, 1, pl.ds(128, 128)], "xp"),
        "t1m0": rdma("t1m0", tb.at[0, 0, pl.ds(0, 128)], tb.at[0, 2, pl.ds(0, 128)], "xm"),
        "t1m1": rdma("t1m1", tb.at[0, 0, pl.ds(128, 128)], tb.at[0, 2, pl.ds(128, 128)], "xm"),
        "trp": rdma("trp", tb.at[0, 1, pl.ds(0, 128)], tb.at[0, 3, pl.ds(0, 128)], "xp"),
        "trm": rdma("trm", tb.at[0, 2, pl.ds(128, 128)], tb.at[0, 3, pl.ds(128, 128)], "xm"),
        "tf0": rdma("tf0", tb.at[0, 0], tb.at[1, 0], "o"),
        "tf1": rdma("tf1", tb.at[0, 1], tb.at[1, 1], "o"),
        "tf2": rdma("tf2", tb.at[0, 2], tb.at[1, 2], "o"),
        "tf3": rdma("tf3", tb.at[0, 3], tb.at[1, 3], "o"),
        "ip": rdma("ip", fd.at[0], fd.at[1], "yp"),
        "im": rdma("im", fd.at[0], fd.at[2], "ym"),
        "i2": rdma("i2", fd.at[0], fd.at[3], "y2"),
        "rp": rdma("rp", rb.at[2], rr.at[0], "yp"),
        "rm": rdma("rm", rb.at[1], rr.at[1], "ym"),
        "r2": rdma("r2", rb.at[3], rr.at[2], "y2"),
        "zp": rdma("zp", dt.at[pl.ds(0, 2), pl.ds(0, 64)], dt.at[pl.ds(0, 2), pl.ds(64, 64)], "zp"),
        "zm": rdma("zm", dt.at[pl.ds(0, 2), pl.ds(0, 64)], dt.at[pl.ds(0, 2), pl.ds(128, 64)], "zm"),
        "z2": rdma("z2", dt.at[pl.ds(0, 2), pl.ds(0, 64)], dt.at[pl.ds(0, 2), pl.ds(192, 64)], "z2"),
        "g2p": rdma("g2p", pb.at[0, pl.ds(0, 2)], gr2.at[0], "zp"),
        "g2m": rdma("g2m", pb.at[0, pl.ds(2, 2)], gr2.at[1], "zm"),
        "gpa": rdma("gpa", pb.at[1, pl.ds(2, 2)], gr.at[0, pl.ds(2, 2)], "zp"),
        "gpb": rdma("gpb", pb.at[1, pl.ds(0, 2)], gr.at[0, pl.ds(0, 2)], "zp"),
        "gma": rdma("gma", pb.at[2, pl.ds(0, 2)], gr.at[1, pl.ds(0, 2)], "zm"),
        "gmb": rdma("gmb", pb.at[2, pl.ds(2, 2)], gr.at[1, pl.ds(2, 2)], "zm"),
    }

    assert len(numbers) == COPIES

    def go(*names):
        for name in names:
            cp[name].start()
            started.append(name)

    def got(*names):
        for name in names:
            cp[name].wait_recv()

    lane = pl.multiple_of((z // 2) * 128, 128)
    small = [
        pltpu.make_async_copy(amp_hbm, am.at[x, y, c], in_sem.at[0]),
        pltpu.make_async_copy(dom_hbm, fd.at[0], in_sem.at[1]),
        pltpu.make_async_copy(fit_hbm.at[:, pl.ds(lane, 128)], fb, in_sem.at[2]),
        pltpu.make_async_copy(list_hbm, list_s, in_sem.at[3]),
        pltpu.make_async_copy(occ_hbm, occ_s, in_sem.at[4]),
        pltpu.make_async_copy(part_hbm, part_s, in_sem.at[5]),
        pltpu.make_async_copy(mask_hbm, mask_s, in_sem.at[6]),
        pltpu.make_async_copy(coup_hbm, coup_s, in_sem.at[7]),
        pltpu.make_async_copy(pen_hbm, pen, in_sem.at[8]),
    ]
    blocks = [z2, zp, zm, z]

    def h_copy(k, o):
        rows = pl.ds(k * 1024, 1024)
        return pltpu.make_async_copy(half_hbm.at[o, rows], hbuf.at[o, rows], h_sem.at[k * 2 + o])

    def c_copy(k):
        return pltpu.make_async_copy(coef_hbm.at[blocks[k]], cbs[k], c_sem.at[k])

    barrier = pltpu.get_barrier_semaphore()
    for place in to.values():
        pl.semaphore_signal(barrier, inc=1, device_id=place, device_id_type=MESH)
    for copy in small:
        copy.start()
    h_copies = [(h_copy(k, 0), h_copy(k, 1)) for k in range(4)]
    for both in h_copies:
        both[0].start()
        both[1].start()
    c_copies = [c_copy(k) for k in range(4)]
    c_copies[0].start()
    inter_copy = pltpu.make_async_copy(inter_hbm, inter, in_sem.at[9])
    small[0].wait()
    small[1].wait()

    pl.semaphore_wait(barrier, len(to))
    go("a1p", "a1m", "b1p", "b1m", "ip", "im", "i2")
    small[2].wait()
    ft[...] = fb[...].T
    side = pl.multiple_of((z % 2) * 64, 64)
    for h in range(4):
        tb[0, 0, h * 64:(h + 1) * 64, :] = ft[pl.ds(side, 64), h * 256:(h + 1) * 256]
    go("t1p0", "t1m1", "tf0")
    small[3].wait()

    def arrange(block):
        label = [list_s[block, 0, p] & 1 for p in range(4)]
        common = jnp.where(label[0] + label[1] + label[2] + label[3] >= 2, 1, 0)
        like = [1 - (one ^ common) for one in label]
        many = like[0] + like[1] + like[2] + like[3]
        seen = 0
        place = []
        for p in range(4):
            place.append(jnp.where(like[p] == 1, seen, many + p - seen))
            seen = seen + like[p]
        pick = [sum(jnp.where(place[p] == j, p, 0) for p in range(1, 4)) for j in range(4)]
        third = jnp.where(many >= 3, common, 1 - common)
        fourth = jnp.where(many == 4, common, 1 - common)
        return common, pick, third, fourth, place

    plans = [arrange(block) for block in blocks]

    def turn(k):
        for o in range(2):
            for i in range(4):
                part = slice(k * 1024 + i * 256, k * 1024 + (i + 1) * 256)
                ht[o, :, part] = hbuf[o, part, :].T

    def wide(block, i, j):
        pick = plans[block][1]
        return jnp.concatenate([cbs[block][pick[i]], cbs[block][pick[j]]], axis=1)

    def dot(a, b):
        return jnp.dot(a, b, preferred_element_type=F32)

    def halves(out):
        return out[:, :128], out[:, 128:]

    def even(block, other):
        first = dot(ht[plans[block][0]], wide(block, 0, 1))
        second = dot(ht[plans[other][0]], wide(other, 0, 1))
        return halves(first), halves(second)

    def mixed(block):
        weights = wide(block, 2, 3)
        zero = dot(ht[0], weights)
        one = dot(ht[1], weights)
        third, fourth = plans[block][2], plans[block][3]
        return (
            jnp.where(third == 1, one[:, :128], zero[:, :128]),
            jnp.where(fourth == 1, one[:, 128:], zero[:, 128:]),
        )

    def keep(slot, at, pair_of, arrived=None):
        for i in range(2):
            value = pair_of[i]
            if arrived is not None:
                value = value + gr2[arrived, i].astype(F32)
            pb[slot, at + i] = value.astype(BF)

    for k in range(4):
        h_copies[k][0].wait()
        h_copies[k][1].wait()
        turn(k)
        if k == 1:
            c_copies[2].start()
    got("a1p")
    go("a1rp")
    got("a1m")
    go("a1rm")
    got("b1p")
    go("b1rp")
    got("b1m")
    go("b1rm")
    go("t1p1", "t1m0")
    c_copies[0].wait()
    c_copies[1].start()
    keep(0, 2, mixed(0))
    go("g2m")
    got("t1p0")
    go("trp")
    got("t1m1")
    go("trm")
    c_copies[2].wait()
    c_copies[3].start()
    inter_copy.start()
    first, second = even(0, 2)
    keep(0, 0, first)
    go("g2p")
    keep(2, 0, second)
    go("gma")
    got("a1rp", "a1rm")
    go("a2p0", "a2m1", "a2p1", "a2m0", "fa1")
    got("b1rp", "b1rm")
    go("b2p0", "b2m1", "b2p1", "b2m0", "fb1")
    c_copies[1].wait()
    keep(1, 2, mixed(1))
    go("gpa")
    got("t1p1")
    go("tf1")
    got("t1m0")
    go("tf2")
    c_copies[3].wait()
    own[2], own[3] = mixed(3)
    got("trp", "trm")
    go("tf3")
    for i in (4, 5, 6, 7, 8):
        small[i].wait()
    for g in range(4):
        occ = occ_s[list_s[z, 0, g]] + occ_s[list_s[z, 1, g]]
        across = jnp.broadcast_to(pen[g:g + 1, :], (128, 128))
        den_ref[g] = (across.T + across) - occ

    got("tf0", "tf1", "tf2", "tf3", "ip", "im", "i2")
    iota = lax.broadcasted_iota(jnp.int32, (256, 256), 0)
    sources = [
        (k, j, (xx * 4 + y) * 2 + cc)
        for k, cc in ((0, c), (1, 1 - c))
        for j, xx in enumerate((x, xm, xp, x2))
    ]

    def select(j):
        for o in range(2):
            wanted = fd[j, o:o + 1, :]
            owner = wanted >> 10
            row = wanted & 255
            quarter = (wanted >> 8) & 3
            total = jnp.zeros((256, 256), F32)
            for k, i, source in sources:
                key = jnp.where(owner == source, row, -1)
                hot = jnp.where(iota == key, 1.0, 0.0).astype(BF)
                total = total + jnp.dot(tb[k, i], hot, preferred_element_type=F32)
            out = jnp.zeros((64, 256), F32)
            for h in range(4):
                out = out + jnp.where(quarter == h, total[h * 64:(h + 1) * 64], 0.0)
            rb[j, o] = out.astype(BF)

    select(3)
    go("r2")
    select(2)
    go("rp")
    got("b2p0")
    go("b2rp")
    got("b2m1")
    go("b2rm")
    select(1)
    go("rm")
    got("a2p0")
    go("a2rp")
    got("a2m1")
    go("a2rm")
    select(0)
    got("g2p")
    first, second = even(1, 3)
    keep(1, 0, first, 0)
    go("gpb")
    own[0], own[1] = second
    got("g2m")
    keep(2, 2, mixed(2), 1)
    go("gmb")
    got("a2p1")
    go("fa2m")
    got("a2m0")
    go("fa2p")
    got("b2p1")
    go("fb2m")
    got("b2m0")
    go("fb2p")
    got("rp", "rm", "r2")
    for o in range(2):
        dt[o, 0:64, :] = (
            (rb[0, o].astype(F32) + rr[0, o].astype(F32)) + (rr[1, o].astype(F32) + rr[2, o].astype(F32))
        ).astype(BF)
    go("z2", "zp", "zm")
    got("a2rp")
    go("fa20")
    got("a2rm")
    go("fa21")
    got("b2rp")
    go("fb20")
    got("b2rm")
    go("fb21")

    got("gpa", "gpb", "gma", "gmb")
    place = plans[3][4]
    factors = [
        (own[place[g]] + gr[0, place[g]].astype(F32) + gr[1, place[g]].astype(F32)).astype(BF) for g in range(4)
    ]
    inter_copy.wait()
    got("fa1", "fb1", "fa2m", "fa2p", "fa20", "fa21", "fb2m", "fb2p", "fb20", "fb21")
    for g in range(4):
        carried = []
        for s in range(8):
            tile = part_s[g, s] & 127
            picked = am[tile >> 5, (tile >> 3) & 3, (tile >> 2) & 1, tile & 3]
            weight = mask_s[g, s].astype(F32) * coup_s[g, s]
            carried.append((weight * dot(inter[g, s], picked)).astype(BF))
        sum_ref[g] = lax.dot_general(
            jnp.concatenate(carried, axis=1),
            jnp.concatenate([inter[g, s] for s in range(8)], axis=1),
            (((1,), (1,)), ((), ())), preferred_element_type=F32,
        )

    got("zp", "zm", "z2")
    fits = [dot(dt[list_s[z, 0, g] & 1], factors[g]).astype(BF) for g in range(4)]
    for g in range(4):
        exchange = lax.dot_general(fits[g], fits[g], (((0,), (0,)), ((), ())), preferred_element_type=F32)
        sum_ref[g] += exchange / 256
    for name in started:
        cp[name].wait_send()


def shards(
    half_ints, pno_coef, pair_list, fit_domain, fit_factor, amplitudes, pno_energy, occ_energy,
    partners, partner_mask, intersections, coupling,
):
    any_spec = pl.BlockSpec(memory_space=pl.ANY)
    vmem_spec = pl.BlockSpec(memory_space=pltpu.VMEM)
    total, denominator = pl.pallas_call(
        kernel,
        out_shape=(
            jax.ShapeDtypeStruct((4, 128, 128), F32),
            jax.ShapeDtypeStruct((4, 128, 128), F32),
        ),
        in_specs=[any_spec] * 12,
        out_specs=(vmem_spec, vmem_spec),
        scratch_shapes=[
            pltpu.VMEM((2, 4096, 256), BF),
            pltpu.VMEM((2, 256, 4096), BF),
        ]
        + [pltpu.VMEM((4, 4096, 128), BF)] * 4
        + [
            pltpu.VMEM((4, 4, 2, 4, 128, 128), BF),
            pltpu.VMEM((1024, 128), BF),
            pltpu.VMEM((128, 1024), BF),
            pltpu.VMEM((2, 4, 256, 256), BF),
            pltpu.VMEM((4, 2, 256), jnp.int32),
            pltpu.VMEM((4, 2, 64, 256), BF),
            pltpu.VMEM((3, 2, 64, 256), BF),
            pltpu.VMEM((2, 256, 256), BF),
            pltpu.VMEM((3, 4, 256, 128), BF),
            pltpu.VMEM((2, 2, 256, 128), BF),
            pltpu.VMEM((2, 4, 256, 128), BF),
            pltpu.VMEM((4, 256, 128), F32),
            pltpu.VMEM((4, 8, 128, 128), BF),
            pltpu.VMEM((4, 128), F32),
            pltpu.SMEM((4, 2, 4), jnp.int32),
            pltpu.SMEM((64,), F32),
            pltpu.SMEM((4, 8), jnp.int32),
            pltpu.SMEM((4, 8), jnp.int32),
            pltpu.SMEM((4, 8), F32),
            pltpu.SemaphoreType.DMA((COPIES,)),
            pltpu.SemaphoreType.DMA((COPIES,)),
            pltpu.SemaphoreType.DMA((8,)),
            pltpu.SemaphoreType.DMA((4,)),
            pltpu.SemaphoreType.DMA((10,)),
        ],
        compiler_params=pltpu.CompilerParams(
            collective_id=0, has_side_effects=True, vmem_limit_bytes=VMEM_LIMIT
        ),
    )(
        half_ints, pno_coef, jnp.swapaxes(pair_list, 1, 2), fit_domain, fit_factor, amplitudes,
        pno_energy, occ_energy, partners, partner_mask, intersections, coupling,
    )
    amps = amplitudes.astype(F32)
    residual = total + denominator * amps
    return residual, (amps - residual / denominator).astype(BF)


def solution(mesh):
    return jax.shard_map(
        shards,
        mesh=mesh,
        in_specs=(
            P("pair", "basis", None),
            P(None, "pair", "basis", None),
            P(None, "pair", None),
            P("pair", None),
            P("pair", None),
            P(("basis", "pair"), None, None),
            P(("basis", "pair"), None),
            P(),
            P(("basis", "pair"), None),
            P(("basis", "pair"), None),
            P(("basis", "pair"), None, None, None),
            P(("basis", "pair"), None),
        ),
        out_specs=(P(("basis", "pair"), None, None), P(("basis", "pair"), None, None)),
        check_vma=False,
    )
```

```python
import jax
import jax.numpy as jnp
from jax import lax
from jax.experimental import pallas as pl
from jax.experimental.pallas import tpu as pltpu
from jax.sharding import PartitionSpec as P

BF = jnp.bfloat16
F32 = jnp.float32
MESH = pl.DeviceIdType.MESH
COPIES = 73
VMEM_LIMIT = 60 * 1024 * 1024


class N:
    (
        t1p0, t1m1, b1p, b1m, ip, im, i2, t1p1, t1m0, a1p,
        a1m, tf0, g2m, trp, trm, b1rp, b1rm, g2p, gma, tf1,
        tf2, gpa, a1rp, a1rm, b2p0, b2m1, b2p1, b2m0, fb1, tf3,
        fa1, gmb, gpb, fa2m, fa2p, fb2m, fb2p, fa20, fa21,
    ) = range(39)
    a2p, a2m, a2rp, a2rm = range(39, 55, 4)
    rp, rm, r2, zp, zm, z2, b2rp, b2rm, fb2 = range(55, 73, 2)


def kernel(
    half_hbm, coef_hbm, list_hbm, dom_hbm, fit_hbm, amp_hbm, pen_hbm, occ_hbm,
    part_hbm, mask_hbm, inter_hbm, coup_hbm,
    sum_ref, den_ref,
    hbuf, ht, cb0, cb1, cb2, cb3,
    am, fb, ft, tb, fd, rb, rr, dt, pb, gr2, gr, own, inter, pen,
    list_s, occ_s, part_s, mask_s, coup_s,
    send_sem, recv_sem, h_sem, c_sem, in_sem,
):
    cbs = (cb0, cb1, cb2, cb3)
    z = lax.axis_index("basis")
    pair = lax.axis_index("pair")
    x, y, c = pair // 8, (pair // 2) % 4, pair % 2
    xp, xm, x2 = (x + 1) % 4, (x + 3) % 4, (x + 2) % 4
    yp, ym, y2 = (y + 1) % 4, (y + 3) % 4, (y + 2) % 4
    zp, zm, z2 = (z + 1) % 4, (z + 3) % 4, (z + 2) % 4

    def dev(zz, xx, yy, cc):
        return (zz, (xx * 4 + yy) * 2 + cc)

    to = {
        "xp": dev(z, xp, y, c), "xm": dev(z, xm, y, c),
        "yp": dev(z, x, yp, c), "ym": dev(z, x, ym, c), "y2": dev(z, x, y2, c),
        "zp": dev(zp, x, y, c), "zm": dev(zm, x, y, c), "z2": dev(z2, x, y, c),
        "o": dev(z, x, y, 1 - c),
    }
    started = []

    def rdma(name, src, dst, where):
        return pltpu.make_async_remote_copy(
            src_ref=src, dst_ref=dst, send_sem=send_sem.at[name], recv_sem=recv_sem.at[name],
            device_id=to[where], device_id_type=MESH,
        )

    def same(name, ref, where):
        return rdma(name, ref, ref, where)

    every = pl.ds(0, 4)
    cp = {
        N.a1p: same(N.a1p, am.at[x, y, c, pl.ds(0, 2)], "xp"),
        N.a1m: same(N.a1m, am.at[x, y, c, pl.ds(0, 2)], "xm"),
        N.a1rp: same(N.a1rp, am.at[xm, y, c, 0], "xp"),
        N.a1rm: same(N.a1rm, am.at[xp, y, c, 1], "xm"),
        N.b1p: same(N.b1p, am.at[x, y, c, pl.ds(2, 2)], "yp"),
        N.b1m: same(N.b1m, am.at[x, y, c, pl.ds(2, 2)], "ym"),
        N.b1rp: same(N.b1rp, am.at[x, ym, c, 2], "yp"),
        N.b1rm: same(N.b1rm, am.at[x, yp, c, 3], "ym"),
        N.b2p0: same(N.b2p0, am.at[x, every, c, 2], "xp"),
        N.b2p1: same(N.b2p1, am.at[x, every, c, 3], "xp"),
        N.b2m0: same(N.b2m0, am.at[x, every, c, 2], "xm"),
        N.b2m1: same(N.b2m1, am.at[x, every, c, 3], "xm"),
        N.fa1: same(N.fa1, am.at[every, y, c, pl.ds(0, 2)], "o"),
        N.fb1: same(N.fb1, am.at[x, every, c, pl.ds(2, 2)], "o"),
        N.fa2m: same(N.fa2m, am.at[every, ym, c, pl.ds(0, 2)], "o"),
        N.fa2p: same(N.fa2p, am.at[every, yp, c, pl.ds(0, 2)], "o"),
        N.fa20: same(N.fa20, am.at[every, y2, c, 0], "o"),
        N.fa21: same(N.fa21, am.at[every, y2, c, 1], "o"),
        N.fb2m: same(N.fb2m, am.at[xm, every, c, pl.ds(2, 2)], "o"),
        N.fb2p: same(N.fb2p, am.at[xp, every, c, pl.ds(2, 2)], "o"),
        N.t1p0: rdma(N.t1p0, tb.at[0, 0, pl.ds(0, 128)], tb.at[0, 1, pl.ds(0, 128)], "xp"),
        N.t1p1: rdma(N.t1p1, tb.at[0, 0, pl.ds(128, 128)], tb.at[0, 1, pl.ds(128, 128)], "xp"),
        N.t1m0: rdma(N.t1m0, tb.at[0, 0, pl.ds(0, 128)], tb.at[0, 2, pl.ds(0, 128)], "xm"),
        N.t1m1: rdma(N.t1m1, tb.at[0, 0, pl.ds(128, 128)], tb.at[0, 2, pl.ds(128, 128)], "xm"),
        N.trp: rdma(N.trp, tb.at[0, 1, pl.ds(0, 128)], tb.at[0, 3, pl.ds(0, 128)], "xp"),
        N.trm: rdma(N.trm, tb.at[0, 2, pl.ds(128, 128)], tb.at[0, 3, pl.ds(128, 128)], "xm"),
        N.tf0: rdma(N.tf0, tb.at[0, 0], tb.at[1, 0], "o"),
        N.tf1: rdma(N.tf1, tb.at[0, 1], tb.at[1, 1], "o"),
        N.tf2: rdma(N.tf2, tb.at[0, 2], tb.at[1, 2], "o"),
        N.tf3: rdma(N.tf3, tb.at[0, 3], tb.at[1, 3], "o"),
        N.ip: rdma(N.ip, fd.at[0], fd.at[1], "yp"),
        N.im: rdma(N.im, fd.at[0], fd.at[2], "ym"),
        N.i2: rdma(N.i2, fd.at[0], fd.at[3], "y2"),
        N.g2p: rdma(N.g2p, pb.at[0, pl.ds(0, 2)], gr2.at[0], "zp"),
        N.g2m: rdma(N.g2m, pb.at[0, pl.ds(2, 2)], gr2.at[1], "zm"),
        N.gpa: rdma(N.gpa, pb.at[1, pl.ds(2, 2)], gr.at[0, pl.ds(2, 2)], "zp"),
        N.gpb: rdma(N.gpb, pb.at[1, pl.ds(0, 2)], gr.at[0, pl.ds(0, 2)], "zp"),
        N.gma: rdma(N.gma, pb.at[2, pl.ds(0, 2)], gr.at[1, pl.ds(0, 2)], "zm"),
        N.gmb: rdma(N.gmb, pb.at[2, pl.ds(2, 2)], gr.at[1, pl.ds(2, 2)], "zm"),
    }

    for j, row in enumerate((x, xm, xp, x2)):
        cp[N.a2p + j] = same(N.a2p + j, am.at[row, y, c, pl.ds(0, 2)], "yp")
        cp[N.a2m + j] = same(N.a2m + j, am.at[row, y, c, pl.ds(0, 2)], "ym")
        cp[N.a2rp + j] = same(N.a2rp + j, am.at[row, ym, c, 0], "yp")
        cp[N.a2rm + j] = same(N.a2rm + j, am.at[row, yp, c, 1], "ym")

    mine = pl.ds(0, 64)
    for o in range(2):
        lines = pl.ds(2 * o, 2)
        cp[N.b2rp + o] = same(N.b2rp + o, am.at[xm, lines, c, 2], "xp")
        cp[N.b2rm + o] = same(N.b2rm + o, am.at[xp, lines, c, 3], "xm")
        cp[N.fb2 + o] = same(N.fb2 + o, am.at[x2, lines, c, pl.ds(2, 2)], "o")
        cp[N.rp + o] = rdma(N.rp + o, rb.at[2, o], rr.at[0, o], "yp")
        cp[N.rm + o] = rdma(N.rm + o, rb.at[1, o], rr.at[1, o], "ym")
        cp[N.r2 + o] = rdma(N.r2 + o, rb.at[3, o], rr.at[2, o], "y2")
        cp[N.zp + o] = rdma(N.zp + o, dt.at[o, mine], dt.at[o, pl.ds(64, 64)], "zp")
        cp[N.zm + o] = rdma(N.zm + o, dt.at[o, mine], dt.at[o, pl.ds(128, 64)], "zm")
        cp[N.z2 + o] = rdma(N.z2 + o, dt.at[o, mine], dt.at[o, pl.ds(192, 64)], "z2")

    def go(*names):
        for name in names:
            cp[name].start()
            started.append(name)

    def got(*names):
        for name in names:
            cp[name].wait_recv()

    lane = pl.multiple_of((z // 2) * 128, 128)
    small = [
        pltpu.make_async_copy(amp_hbm, am.at[x, y, c], in_sem.at[0]),
        pltpu.make_async_copy(dom_hbm, fd.at[0], in_sem.at[1]),
        pltpu.make_async_copy(fit_hbm.at[:, pl.ds(lane, 128)], fb, in_sem.at[2]),
        pltpu.make_async_copy(list_hbm, list_s, in_sem.at[3]),
        pltpu.make_async_copy(occ_hbm, occ_s, in_sem.at[4]),
        pltpu.make_async_copy(part_hbm, part_s, in_sem.at[5]),
        pltpu.make_async_copy(mask_hbm, mask_s, in_sem.at[6]),
        pltpu.make_async_copy(coup_hbm, coup_s, in_sem.at[7]),
        pltpu.make_async_copy(pen_hbm, pen, in_sem.at[8]),
    ]
    blocks = [z2, zp, zm, z]

    def h_copy(k, o):
        rows = pl.ds(k * 1024, 1024)
        return pltpu.make_async_copy(half_hbm.at[o, rows], hbuf.at[o, rows], h_sem.at[k * 2 + o])

    def c_copy(k):
        return pltpu.make_async_copy(coef_hbm.at[blocks[k]], cbs[k], c_sem.at[k])

    barrier = pltpu.get_barrier_semaphore()
    for place in to.values():
        pl.semaphore_signal(barrier, inc=1, device_id=place, device_id_type=MESH)
    for copy in small:
        copy.start()
    h_copies = [(h_copy(k, 0), h_copy(k, 1)) for k in range(4)]
    for both in h_copies:
        both[0].start()
        both[1].start()
    c_copies = [c_copy(k) for k in range(4)]
    c_copies[0].start()
    inter_copy = pltpu.make_async_copy(inter_hbm, inter, in_sem.at[9])
    small[0].wait()
    small[1].wait()

    small[2].wait()
    ft[...] = fb[...].T
    side = pl.multiple_of((z % 2) * 64, 64)
    for h in range(4):
        tb[0, 0, h * 64:(h + 1) * 64, :] = ft[pl.ds(side, 64), h * 256:(h + 1) * 256]
    pl.semaphore_wait(barrier, len(to))
    go(N.t1p0, N.t1m1, N.b1p, N.b1m, N.ip, N.im, N.i2, N.t1p1, N.t1m0, N.a1p, N.a1m, N.a2p + 0, N.a2m + 0, N.tf0)
    small[3].wait()

    def arrange(block):
        label = [list_s[block, 0, p] & 1 for p in range(4)]
        common = jnp.where(label[0] + label[1] + label[2] + label[3] >= 2, 1, 0)
        like = [1 - (one ^ common) for one in label]
        many = like[0] + like[1] + like[2] + like[3]
        seen = 0
        place = []
        for p in range(4):
            place.append(jnp.where(like[p] == 1, seen, many + p - seen))
            seen = seen + like[p]
        pick = [sum(jnp.where(place[p] == j, p, 0) for p in range(1, 4)) for j in range(4)]
        third = jnp.where(many >= 3, common, 1 - common)
        fourth = jnp.where(many == 4, common, 1 - common)
        return common, pick, third, fourth, place

    plans = [arrange(block) for block in blocks]

    def turn(k):
        for o in range(2):
            for i in range(4):
                part = slice(k * 1024 + i * 256, k * 1024 + (i + 1) * 256)
                ht[o, :, part] = hbuf[o, part, :].T

    def wide(block, i, j):
        pick = plans[block][1]
        return jnp.concatenate([cbs[block][pick[i]], cbs[block][pick[j]]], axis=1)

    def dot(a, b):
        return jnp.dot(a, b, preferred_element_type=F32)

    def halves(out):
        return out[:, :128], out[:, 128:]

    def even(block, other):
        first = dot(ht[plans[block][0]], wide(block, 0, 1))
        second = dot(ht[plans[other][0]], wide(other, 0, 1))
        return halves(first), halves(second)

    def mixed(block):
        weights = wide(block, 2, 3)
        zero = dot(ht[0], weights)
        one = dot(ht[1], weights)
        third, fourth = plans[block][2], plans[block][3]
        return (
            jnp.where(third == 1, one[:, :128], zero[:, :128]),
            jnp.where(fourth == 1, one[:, 128:], zero[:, 128:]),
        )

    def keep(slot, at, pair_of, arrived=None):
        for i in range(2):
            value = pair_of[i]
            if arrived is not None:
                value = value + gr2[arrived, i].astype(F32)
            pb[slot, at + i] = value.astype(BF)

    for k in range(4):
        h_copies[k][0].wait()
        h_copies[k][1].wait()
        turn(k)
        if k == 1:
            c_copies[2].start()
    c_copies[0].wait()
    c_copies[1].start()
    keep(0, 2, mixed(0))
    go(N.g2m)
    got(N.t1p0)
    go(N.trp)
    got(N.t1m1)
    go(N.trm)
    got(N.b1p)
    go(N.b1rp)
    got(N.b1m)
    go(N.b1rm)
    c_copies[2].wait()
    c_copies[3].start()
    inter_copy.start()
    first, second = even(0, 2)
    keep(0, 0, first)
    go(N.g2p)
    keep(2, 0, second)
    go(N.gma)
    got(N.a2p + 0)
    go(N.a2rp + 0)
    got(N.a2m + 0)
    go(N.a2rm + 0)
    got(N.t1p1)
    go(N.tf1)
    got(N.t1m0)
    go(N.tf2)
    c_copies[1].wait()
    keep(1, 2, mixed(1))
    go(N.gpa)
    got(N.a1p)
    go(N.a1rp, N.a2p + 1, N.a2m + 1)
    got(N.a1m)
    go(N.a1rm, N.a2p + 2, N.a2m + 2)
    got(N.b1rp, N.b1rm)
    go(N.b2p0, N.b2m1, N.b2p1, N.b2m0, N.fb1)
    got(N.trp, N.trm)
    go(N.tf3)
    c_copies[3].wait()
    first, second = even(1, 3)
    own[0], own[1] = second
    third = mixed(2)
    got(N.a1rp, N.a1rm)
    go(N.a2p + 3, N.a2m + 3, N.fa1)
    got(N.g2m)
    keep(2, 2, third, 1)
    go(N.gmb)
    got(N.g2p)
    keep(1, 0, first, 0)
    go(N.gpb)

    got(N.tf0, N.tf1, N.tf2, N.tf3, N.ip, N.im, N.i2)
    iota = lax.broadcasted_iota(jnp.int32, (256, 256), 0)
    sources = [
        (k, j, (xx * 4 + y) * 2 + cc)
        for k, cc in ((0, c), (1, 1 - c))
        for j, xx in enumerate((x, xm, xp, x2))
    ]

    def select(*wanted_of):
        parts = []
        for j, o in wanted_of:
            wanted = fd[j, o:o + 1, :]
            parts.append((wanted >> 10, wanted & 255, (wanted >> 8) & 3))
        totals = [jnp.zeros((256, 256), F32) for _ in parts]
        for k, i, source in sources:
            for n, (owner, row, _) in enumerate(parts):
                key = jnp.where(owner == source, row, -1)
                hot = jnp.where(iota == key, 1.0, 0.0).astype(BF)
                totals[n] = totals[n] + dot(tb[k, i], hot)
        for n, (j, o) in enumerate(wanted_of):
            out = jnp.zeros((64, 256), F32)
            for h in range(4):
                out = out + jnp.where(parts[n][2] == h, totals[n][h * 64:(h + 1) * 64], 0.0)
            rb[j, o] = out.astype(BF)

    def rows(o):
        got(N.rp + o, N.rm + o, N.r2 + o)
        dt[o, 0:64, :] = (
            (rb[0, o].astype(F32) + rr[0, o].astype(F32)) + (rr[1, o].astype(F32) + rr[2, o].astype(F32))
        ).astype(BF)
        go(N.z2 + o, N.zp + o, N.zm + o)

    select((3, 0), (2, 0))
    go(N.r2 + 0, N.rp + 0)
    select((1, 0), (3, 1))
    go(N.rm + 0, N.r2 + 1)
    got(N.b2p0)
    go(N.b2rp + 0, N.b2rp + 1)
    got(N.b2m1)
    go(N.b2rm + 0, N.b2rm + 1)
    select((2, 1), (1, 1))
    go(N.rp + 1, N.rm + 1)
    for j in (1, 2):
        got(N.a2p + j)
        go(N.a2rp + j)
        got(N.a2m + j)
        go(N.a2rm + j)
    select((0, 0), (0, 1))
    got(N.a2p + 3)
    go(N.a2rp + 3, N.fa2m)
    got(N.a2m + 3)
    go(N.a2rm + 3, N.fa2p)
    own[2], own[3] = mixed(3)
    got(N.b2p1)
    go(N.fb2m)
    got(N.b2m0)
    go(N.fb2p)
    rows(0)
    rows(1)
    for i in (4, 5, 6, 7, 8):
        small[i].wait()
    for g in range(4):
        occ = occ_s[list_s[z, 0, g]] + occ_s[list_s[z, 1, g]]
        across = jnp.broadcast_to(pen[g:g + 1, :], (128, 128))
        den_ref[g] = (across.T + across) - occ
    got(N.a2rp + 0, N.a2rp + 1, N.a2rp + 2, N.a2rp + 3)
    go(N.fa20)
    got(N.a2rm + 0, N.a2rm + 1, N.a2rm + 2, N.a2rm + 3)
    go(N.fa21)
    for o in range(2):
        got(N.b2rp + o, N.b2rm + o)
        go(N.fb2 + o)

    got(N.gpa, N.gpb, N.gma, N.gmb)
    place = plans[3][4]
    factors = [
        (own[place[g]] + gr[0, place[g]].astype(F32) + gr[1, place[g]].astype(F32)).astype(BF) for g in range(4)
    ]
    inter_copy.wait()
    got(N.fa1, N.fb1, N.fa2m, N.fa2p, N.fa20, N.fa21, N.fb2m, N.fb2p, N.fb2 + 0, N.fb2 + 1)
    for g in range(4):
        carried = []
        for s in range(8):
            tile = part_s[g, s] & 127
            picked = am[tile >> 5, (tile >> 3) & 3, (tile >> 2) & 1, tile & 3]
            weight = mask_s[g, s].astype(F32) * coup_s[g, s]
            carried.append((weight * dot(inter[g, s], picked)).astype(BF))
        sum_ref[g] = lax.dot_general(
            jnp.concatenate(carried, axis=1),
            jnp.concatenate([inter[g, s] for s in range(8)], axis=1),
            (((1,), (1,)), ((), ())), preferred_element_type=F32,
        )

    got(N.zp + 0, N.zm + 0, N.z2 + 0, N.zp + 1, N.zm + 1, N.z2 + 1)
    fits = [dot(dt[list_s[z, 0, g] & 1], factors[g]).astype(BF) for g in range(4)]
    for g in range(4):
        exchange = lax.dot_general(fits[g], fits[g], (((0,), (0,)), ((), ())), preferred_element_type=F32)
        sum_ref[g] += exchange / 256
    for name in started:
        cp[name].wait_send()


def shards(
    half_ints, pno_coef, pair_list, fit_domain, fit_factor, amplitudes, pno_energy, occ_energy,
    partners, partner_mask, intersections, coupling,
):
    any_spec = pl.BlockSpec(memory_space=pl.ANY)
    vmem_spec = pl.BlockSpec(memory_space=pltpu.VMEM)
    total, denominator = pl.pallas_call(
        kernel,
        out_shape=(
            pltpu.VMEM((4, 128, 128), F32),
            pltpu.VMEM((4, 128, 128), F32),
        ),
        in_specs=[any_spec] * 12,
        out_specs=(vmem_spec, vmem_spec),
        scratch_shapes=[
            pltpu.VMEM((2, 4096, 256), BF),
            pltpu.VMEM((2, 256, 4096), BF),
        ]
        + [pltpu.VMEM((4, 4096, 128), BF)] * 4
        + [
            pltpu.VMEM((4, 4, 2, 4, 128, 128), BF),
            pltpu.VMEM((1024, 128), BF),
            pltpu.VMEM((128, 1024), BF),
            pltpu.VMEM((2, 4, 256, 256), BF),
            pltpu.VMEM((4, 2, 256), jnp.int32),
            pltpu.VMEM((4, 2, 64, 256), BF),
            pltpu.VMEM((3, 2, 64, 256), BF),
            pltpu.VMEM((2, 256, 256), BF),
            pltpu.VMEM((3, 4, 256, 128), BF),
            pltpu.VMEM((2, 2, 256, 128), BF),
            pltpu.VMEM((2, 4, 256, 128), BF),
            pltpu.VMEM((4, 256, 128), F32),
            pltpu.VMEM((4, 8, 128, 128), BF),
            pltpu.VMEM((4, 128), F32),
            pltpu.SMEM((4, 2, 4), jnp.int32),
            pltpu.SMEM((64,), F32),
            pltpu.SMEM((4, 8), jnp.int32),
            pltpu.SMEM((4, 8), jnp.int32),
            pltpu.SMEM((4, 8), F32),
            pltpu.SemaphoreType.DMA((COPIES,)),
            pltpu.SemaphoreType.DMA((COPIES,)),
            pltpu.SemaphoreType.DMA((8,)),
            pltpu.SemaphoreType.DMA((4,)),
            pltpu.SemaphoreType.DMA((10,)),
        ],
        compiler_params=pltpu.CompilerParams(
            collective_id=0, has_side_effects=True, vmem_limit_bytes=VMEM_LIMIT
        ),
    )(
        half_ints, pno_coef, jnp.swapaxes(pair_list, 1, 2), fit_domain, fit_factor, amplitudes,
        pno_energy, occ_energy, partners, partner_mask, intersections, coupling,
    )
    amps = amplitudes.astype(F32)
    residual = total + denominator * amps
    return residual, (amps - residual / denominator).astype(BF)


def solution(mesh):
    return jax.shard_map(
        shards,
        mesh=mesh,
        in_specs=(
            P("pair", "basis", None),
            P(None, "pair", "basis", None),
            P(None, "pair", None),
            P("pair", None),
            P("pair", None),
            P(("basis", "pair"), None, None),
            P(("basis", "pair"), None),
            P(),
            P(("basis", "pair"), None),
            P(("basis", "pair"), None),
            P(("basis", "pair"), None, None, None),
            P(("basis", "pair"), None),
        ),
        out_specs=(P(("basis", "pair"), None, None), P(("basis", "pair"), None, None)),
        check_vma=False,
    )
```

```python
import jax
import jax.numpy as jnp
from jax import lax
from jax.experimental import pallas as pl
from jax.experimental.pallas import tpu as pltpu
from jax.sharding import PartitionSpec as P

BF = jnp.bfloat16
F32 = jnp.float32
MESH = pl.DeviceIdType.MESH
COPIES = 73
VMEM_LIMIT = 60 * 1024 * 1024


class N:
    (
        t1p0, t1m1, b1p, b1m, ip, im, i2, t1p1, t1m0, a1p,
        a1m, tf0, g2m, trp, trm, b1rp, b1rm, g2p, gma, tf1,
        tf2, gpa, a1rp, a1rm, b2p0, b2m1, b2p1, b2m0, fb1, tf3,
        fa1, gmb, gpb, fa2m, fa2p, fb2m, fb2p, fa20, fa21,
    ) = range(39)
    a2p, a2m, a2rp, a2rm = range(39, 55, 4)
    rp, rm, r2, zp, zm, z2, b2rp, b2rm, fb2 = range(55, 73, 2)


def kernel(
    half_hbm, coef_hbm, list_hbm, dom_hbm, fit_hbm, amp_hbm, pen_hbm, occ_hbm,
    part_hbm, mask_hbm, inter_hbm, coup_hbm,
    sum_ref, den_ref,
    hbuf, ht, cb0, cb1, cb2, cb3,
    am, fb, ft, tb, fd, rb, rr, dt, pb, gr2, gr, own, inter, pen,
    list_s, occ_s, part_s, mask_s, coup_s,
    send_sem, recv_sem, h_sem, c_sem, in_sem,
):
    cbs = (cb0, cb1, cb2, cb3)
    z = lax.axis_index("basis")
    pair = lax.axis_index("pair")
    x, y, c = pair // 8, (pair // 2) % 4, pair % 2
    xp, xm, x2 = (x + 1) % 4, (x + 3) % 4, (x + 2) % 4
    yp, ym, y2 = (y + 1) % 4, (y + 3) % 4, (y + 2) % 4
    zp, zm, z2 = (z + 1) % 4, (z + 3) % 4, (z + 2) % 4

    def dev(zz, xx, yy, cc):
        return (zz, (xx * 4 + yy) * 2 + cc)

    to = {
        "xp": dev(z, xp, y, c), "xm": dev(z, xm, y, c),
        "yp": dev(z, x, yp, c), "ym": dev(z, x, ym, c), "y2": dev(z, x, y2, c),
        "zp": dev(zp, x, y, c), "zm": dev(zm, x, y, c), "z2": dev(z2, x, y, c),
        "o": dev(z, x, y, 1 - c),
    }
    started = []

    def rdma(name, src, dst, where):
        return pltpu.make_async_remote_copy(
            src_ref=src, dst_ref=dst, send_sem=send_sem.at[name], recv_sem=recv_sem.at[name],
            device_id=to[where], device_id_type=MESH,
        )

    def same(name, ref, where):
        return rdma(name, ref, ref, where)

    every = pl.ds(0, 4)
    cp = {
        N.a1p: same(N.a1p, am.at[x, y, c, pl.ds(0, 2)], "xp"),
        N.a1m: same(N.a1m, am.at[x, y, c, pl.ds(0, 2)], "xm"),
        N.a1rp: same(N.a1rp, am.at[xm, y, c, 0], "xp"),
        N.a1rm: same(N.a1rm, am.at[xp, y, c, 1], "xm"),
        N.b1p: same(N.b1p, am.at[x, y, c, pl.ds(2, 2)], "yp"),
        N.b1m: same(N.b1m, am.at[x, y, c, pl.ds(2, 2)], "ym"),
        N.b1rp: same(N.b1rp, am.at[x, ym, c, 2], "yp"),
        N.b1rm: same(N.b1rm, am.at[x, yp, c, 3], "ym"),
        N.b2p0: same(N.b2p0, am.at[x, every, c, 2], "xp"),
        N.b2p1: same(N.b2p1, am.at[x, every, c, 3], "xp"),
        N.b2m0: same(N.b2m0, am.at[x, every, c, 2], "xm"),
        N.b2m1: same(N.b2m1, am.at[x, every, c, 3], "xm"),
        N.fa1: same(N.fa1, am.at[every, y, c, pl.ds(0, 2)], "o"),
        N.fb1: same(N.fb1, am.at[x, every, c, pl.ds(2, 2)], "o"),
        N.fa2m: same(N.fa2m, am.at[every, ym, c, pl.ds(0, 2)], "o"),
        N.fa2p: same(N.fa2p, am.at[every, yp, c, pl.ds(0, 2)], "o"),
        N.fa20: same(N.fa20, am.at[every, y2, c, 0], "o"),
        N.fa21: same(N.fa21, am.at[every, y2, c, 1], "o"),
        N.fb2m: same(N.fb2m, am.at[xm, every, c, pl.ds(2, 2)], "o"),
        N.fb2p: same(N.fb2p, am.at[xp, every, c, pl.ds(2, 2)], "o"),
        N.t1p0: rdma(N.t1p0, tb.at[0, 0, pl.ds(0, 128)], tb.at[0, 1, pl.ds(0, 128)], "xp"),
        N.t1p1: rdma(N.t1p1, tb.at[0, 0, pl.ds(128, 128)], tb.at[0, 1, pl.ds(128, 128)], "xp"),
        N.t1m0: rdma(N.t1m0, tb.at[0, 0, pl.ds(0, 128)], tb.at[0, 2, pl.ds(0, 128)], "xm"),
        N.t1m1: rdma(N.t1m1, tb.at[0, 0, pl.ds(128, 128)], tb.at[0, 2, pl.ds(128, 128)], "xm"),
        N.trp: rdma(N.trp, tb.at[0, 1, pl.ds(0, 128)], tb.at[0, 3, pl.ds(0, 128)], "xp"),
        N.trm: rdma(N.trm, tb.at[0, 2, pl.ds(128, 128)], tb.at[0, 3, pl.ds(128, 128)], "xm"),
        N.tf0: rdma(N.tf0, tb.at[0, 0], tb.at[1, 0], "o"),
        N.tf1: rdma(N.tf1, tb.at[0, 1], tb.at[1, 1], "o"),
        N.tf2: rdma(N.tf2, tb.at[0, 2], tb.at[1, 2], "o"),
        N.tf3: rdma(N.tf3, tb.at[0, 3], tb.at[1, 3], "o"),
        N.ip: rdma(N.ip, fd.at[0], fd.at[1], "yp"),
        N.im: rdma(N.im, fd.at[0], fd.at[2], "ym"),
        N.i2: rdma(N.i2, fd.at[0], fd.at[3], "y2"),
        N.g2p: rdma(N.g2p, pb.at[0, pl.ds(0, 2)], gr2.at[0], "zp"),
        N.g2m: rdma(N.g2m, pb.at[0, pl.ds(2, 2)], gr2.at[1], "zm"),
        N.gpa: rdma(N.gpa, pb.at[1, pl.ds(2, 2)], gr.at[0, pl.ds(2, 2)], "zp"),
        N.gpb: rdma(N.gpb, pb.at[1, pl.ds(0, 2)], gr.at[0, pl.ds(0, 2)], "zp"),
        N.gma: rdma(N.gma, pb.at[2, pl.ds(0, 2)], gr.at[1, pl.ds(0, 2)], "zm"),
        N.gmb: rdma(N.gmb, pb.at[2, pl.ds(2, 2)], gr.at[1, pl.ds(2, 2)], "zm"),
    }

    for j, row in enumerate((x, xm, xp, x2)):
        cp[N.a2p + j] = same(N.a2p + j, am.at[row, y, c, pl.ds(0, 2)], "yp")
        cp[N.a2m + j] = same(N.a2m + j, am.at[row, y, c, pl.ds(0, 2)], "ym")
        cp[N.a2rp + j] = same(N.a2rp + j, am.at[row, ym, c, 0], "yp")
        cp[N.a2rm + j] = same(N.a2rm + j, am.at[row, yp, c, 1], "ym")

    mine = pl.ds(0, 64)
    for o in range(2):
        lines = pl.ds(2 * o, 2)
        cp[N.b2rp + o] = same(N.b2rp + o, am.at[xm, lines, c, 2], "xp")
        cp[N.b2rm + o] = same(N.b2rm + o, am.at[xp, lines, c, 3], "xm")
        cp[N.fb2 + o] = same(N.fb2 + o, am.at[x2, lines, c, pl.ds(2, 2)], "o")
        cp[N.rp + o] = rdma(N.rp + o, rb.at[2, o], rr.at[0, o], "yp")
        cp[N.rm + o] = rdma(N.rm + o, rb.at[1, o], rr.at[1, o], "ym")
        cp[N.r2 + o] = rdma(N.r2 + o, rb.at[3, o], rr.at[2, o], "y2")
        cp[N.zp + o] = rdma(N.zp + o, dt.at[o, mine], dt.at[o, pl.ds(64, 64)], "zp")
        cp[N.zm + o] = rdma(N.zm + o, dt.at[o, mine], dt.at[o, pl.ds(128, 64)], "zm")
        cp[N.z2 + o] = rdma(N.z2 + o, dt.at[o, mine], dt.at[o, pl.ds(192, 64)], "z2")

    def go(*names):
        for name in names:
            cp[name].start()
            started.append(name)

    def got(*names):
        for name in names:
            cp[name].wait_recv()

    lane = pl.multiple_of((z // 2) * 128, 128)
    small = [
        pltpu.make_async_copy(amp_hbm, am.at[x, y, c], in_sem.at[0]),
        pltpu.make_async_copy(dom_hbm, fd.at[0], in_sem.at[1]),
        pltpu.make_async_copy(fit_hbm.at[:, pl.ds(lane, 128)], fb, in_sem.at[2]),
        pltpu.make_async_copy(list_hbm, list_s, in_sem.at[3]),
        pltpu.make_async_copy(occ_hbm, occ_s, in_sem.at[4]),
        pltpu.make_async_copy(part_hbm, part_s, in_sem.at[5]),
        pltpu.make_async_copy(mask_hbm, mask_s, in_sem.at[6]),
        pltpu.make_async_copy(coup_hbm, coup_s, in_sem.at[7]),
        pltpu.make_async_copy(pen_hbm, pen, in_sem.at[8]),
    ]
    blocks = [z2, zp, zm, z]

    def h_copy(k, o):
        rows = pl.ds(k * 1024, 1024)
        return pltpu.make_async_copy(half_hbm.at[o, rows], hbuf.at[o, rows], h_sem.at[k * 2 + o])

    def c_copy(k):
        return pltpu.make_async_copy(coef_hbm.at[blocks[k]], cbs[k], c_sem.at[k])

    barrier = pltpu.get_barrier_semaphore()
    for place in to.values():
        pl.semaphore_signal(barrier, inc=1, device_id=place, device_id_type=MESH)
    for i in (2, 0, 1, 3, 4, 5, 6, 7, 8):
        small[i].start()
    h_copies = [(h_copy(k, 0), h_copy(k, 1)) for k in range(4)]
    for both in h_copies:
        both[0].start()
        both[1].start()
    c_copies = [c_copy(k) for k in range(4)]
    c_copies[0].start()
    inter_copy = pltpu.make_async_copy(inter_hbm, inter, in_sem.at[9])

    small[2].wait()
    ft[...] = fb[...].T
    side = pl.multiple_of((z % 2) * 64, 64)
    for h in range(4):
        tb[0, 0, h * 64:(h + 1) * 64, :] = ft[pl.ds(side, 64), h * 256:(h + 1) * 256]
    small[0].wait()
    small[1].wait()
    pl.semaphore_wait(barrier, len(to))
    go(N.t1p0, N.t1m1, N.b1p, N.b1m, N.ip, N.im, N.i2, N.t1p1, N.t1m0, N.a1p, N.a1m, N.a2p + 0, N.a2m + 0, N.tf0)
    small[3].wait()

    def arrange(block):
        label = [list_s[block, 0, p] & 1 for p in range(4)]
        common = jnp.where(label[0] + label[1] + label[2] + label[3] >= 2, 1, 0)
        like = [1 - (one ^ common) for one in label]
        many = like[0] + like[1] + like[2] + like[3]
        seen = 0
        place = []
        for p in range(4):
            place.append(jnp.where(like[p] == 1, seen, many + p - seen))
            seen = seen + like[p]
        pick = [sum(jnp.where(place[p] == j, p, 0) for p in range(1, 4)) for j in range(4)]
        third = jnp.where(many >= 3, common, 1 - common)
        fourth = jnp.where(many == 4, common, 1 - common)
        return common, pick, third, fourth, place

    plans = [arrange(block) for block in blocks]

    def turn(k):
        for o in range(2):
            for i in range(4):
                part = slice(k * 1024 + i * 256, k * 1024 + (i + 1) * 256)
                ht[o, :, part] = hbuf[o, part, :].T

    def wide(block, i, j):
        pick = plans[block][1]
        return jnp.concatenate([cbs[block][pick[i]], cbs[block][pick[j]]], axis=1)

    def dot(a, b):
        return jnp.dot(a, b, preferred_element_type=F32)

    def halves(out):
        return out[:, :128], out[:, 128:]

    def even(block, other):
        first = dot(ht[plans[block][0]], wide(block, 0, 1))
        second = dot(ht[plans[other][0]], wide(other, 0, 1))
        return halves(first), halves(second)

    def mixed(block):
        weights = wide(block, 2, 3)
        zero = dot(ht[0], weights)
        one = dot(ht[1], weights)
        third, fourth = plans[block][2], plans[block][3]
        return (
            jnp.where(third == 1, one[:, :128], zero[:, :128]),
            jnp.where(fourth == 1, one[:, 128:], zero[:, 128:]),
        )

    def keep(slot, at, pair_of, arrived=None):
        for i in range(2):
            value = pair_of[i]
            if arrived is not None:
                value = value + gr2[arrived, i].astype(F32)
            pb[slot, at + i] = value.astype(BF)

    for k in range(4):
        h_copies[k][0].wait()
        h_copies[k][1].wait()
        turn(k)
        if k == 1:
            c_copies[2].start()
    c_copies[0].wait()
    c_copies[1].start()
    keep(0, 2, mixed(0))
    go(N.g2m)
    got(N.t1p0)
    go(N.trp)
    got(N.t1m1)
    go(N.trm)
    got(N.b1p)
    go(N.b1rp)
    got(N.b1m)
    go(N.b1rm)
    c_copies[2].wait()
    c_copies[3].start()
    inter_copy.start()
    first, second = even(0, 2)
    keep(0, 0, first)
    go(N.g2p)
    keep(2, 0, second)
    go(N.gma)
    got(N.a2p + 0)
    go(N.a2rp + 0)
    got(N.a2m + 0)
    go(N.a2rm + 0)
    got(N.t1p1)
    go(N.tf1)
    got(N.t1m0)
    go(N.tf2)
    c_copies[1].wait()
    keep(1, 2, mixed(1))
    go(N.gpa)
    got(N.a1p)
    go(N.a1rp, N.a2p + 1, N.a2m + 1)
    got(N.a1m)
    go(N.a1rm, N.a2p + 2, N.a2m + 2)
    got(N.b1rp, N.b1rm)
    go(N.b2p0, N.b2m1, N.b2p1, N.b2m0, N.fb1)
    got(N.trp, N.trm)
    go(N.tf3)
    c_copies[3].wait()
    first, second = even(1, 3)
    own[0], own[1] = second
    third = mixed(2)
    got(N.a1rp, N.a1rm)
    go(N.a2p + 3, N.a2m + 3, N.fa1)
    got(N.g2m)
    keep(2, 2, third, 1)
    go(N.gmb)
    got(N.g2p)
    keep(1, 0, first, 0)
    go(N.gpb)

    got(N.tf0, N.tf1, N.tf2, N.tf3, N.ip, N.im, N.i2)
    iota = lax.broadcasted_iota(jnp.int32, (256, 256), 0)
    sources = [
        (k, j, (xx * 4 + y) * 2 + cc)
        for k, cc in ((0, c), (1, 1 - c))
        for j, xx in enumerate((x, xm, xp, x2))
    ]

    def select(*wanted_of):
        parts = []
        for j, o in wanted_of:
            wanted = fd[j, o:o + 1, :]
            parts.append((wanted >> 10, wanted & 255, (wanted >> 8) & 3))
        totals = [jnp.zeros((256, 256), F32) for _ in parts]
        for k, i, source in sources:
            for n, (owner, row, _) in enumerate(parts):
                key = jnp.where(owner == source, row, -1)
                hot = jnp.where(iota == key, 1.0, 0.0).astype(BF)
                totals[n] = totals[n] + dot(tb[k, i], hot)
        for n, (j, o) in enumerate(wanted_of):
            out = jnp.zeros((64, 256), F32)
            for h in range(4):
                out = out + jnp.where(parts[n][2] == h, totals[n][h * 64:(h + 1) * 64], 0.0)
            rb[j, o] = out.astype(BF)

    def rows(o):
        got(N.rp + o, N.rm + o, N.r2 + o)
        dt[o, 0:64, :] = (
            (rb[0, o].astype(F32) + rr[0, o].astype(F32)) + (rr[1, o].astype(F32) + rr[2, o].astype(F32))
        ).astype(BF)
        go(N.z2 + o, N.zp + o, N.zm + o)

    select((3, 0), (2, 0))
    go(N.r2 + 0, N.rp + 0)
    select((1, 0), (3, 1))
    go(N.rm + 0, N.r2 + 1)
    got(N.b2p0)
    go(N.b2rp + 0, N.b2rp + 1)
    got(N.b2m1)
    go(N.b2rm + 0, N.b2rm + 1)
    select((2, 1), (1, 1))
    go(N.rp + 1, N.rm + 1)
    for j in (1, 2):
        got(N.a2p + j)
        go(N.a2rp + j)
        got(N.a2m + j)
        go(N.a2rm + j)
    select((0, 0), (0, 1))
    got(N.a2p + 3)
    go(N.a2rp + 3, N.fa2m)
    got(N.a2m + 3)
    go(N.a2rm + 3, N.fa2p)
    own[2], own[3] = mixed(3)
    got(N.b2p1)
    go(N.fb2m)
    got(N.b2m0)
    go(N.fb2p)
    rows(0)
    rows(1)
    for i in (4, 5, 6, 7, 8):
        small[i].wait()
    for g in range(4):
        occ = occ_s[list_s[z, 0, g]] + occ_s[list_s[z, 1, g]]
        across = jnp.broadcast_to(pen[g:g + 1, :], (128, 128))
        den_ref[g] = (across.T + across) - occ
    got(N.a2rp + 0, N.a2rp + 1, N.a2rp + 2, N.a2rp + 3)
    go(N.fa20)
    got(N.a2rm + 0, N.a2rm + 1, N.a2rm + 2, N.a2rm + 3)
    go(N.fa21)
    for o in range(2):
        got(N.b2rp + o, N.b2rm + o)
        go(N.fb2 + o)

    got(N.gpa, N.gpb, N.gma, N.gmb)
    place = plans[3][4]
    factors = [
        (own[place[g]] + gr[0, place[g]].astype(F32) + gr[1, place[g]].astype(F32)).astype(BF) for g in range(4)
    ]
    inter_copy.wait()

    @pl.when(c == 0)
    def _():
        got(N.fa1, N.fb1, N.fa2m, N.fa2p, N.fa20, N.fa21, N.fb2m, N.fb2p, N.fb2 + 0, N.fb2 + 1)
        for g in range(4):
            carried = []
            for s in range(8):
                tile = part_s[g, s] & 127
                picked = am[tile >> 5, (tile >> 3) & 3, (tile >> 2) & 1, tile & 3]
                weight = mask_s[g, s].astype(F32) * coup_s[g, s]
                carried.append((weight * dot(inter[g, s], picked)).astype(BF))
            sum_ref[g] = lax.dot_general(
                jnp.concatenate(carried, axis=1),
                jnp.concatenate([inter[g, s] for s in range(8)], axis=1),
                (((1,), (1,)), ((), ())), preferred_element_type=F32,
            )

        got(N.zp + 0, N.zm + 0, N.z2 + 0, N.zp + 1, N.zm + 1, N.z2 + 1)
        fits = [dot(dt[list_s[z, 0, g] & 1], factors[g]).astype(BF) for g in range(4)]
        for g in range(4):
            exchange = lax.dot_general(fits[g], fits[g], (((0,), (0,)), ((), ())), preferred_element_type=F32)
            sum_ref[g] += exchange / 256

    @pl.when(c == 1)
    def _():
        got(N.zp + 0, N.zm + 0, N.z2 + 0, N.zp + 1, N.zm + 1, N.z2 + 1)
        fits = [dot(dt[list_s[z, 0, g] & 1], factors[g]).astype(BF) for g in range(4)]
        for g in range(4):
            exchange = lax.dot_general(fits[g], fits[g], (((0,), (0,)), ((), ())), preferred_element_type=F32)
            sum_ref[g] = exchange / 256
        got(N.fa1, N.fb1, N.fa2m, N.fa2p, N.fa20, N.fa21, N.fb2m, N.fb2p, N.fb2 + 0, N.fb2 + 1)
        for g in range(4):
            carried = []
            for s in range(8):
                tile = part_s[g, s] & 127
                picked = am[tile >> 5, (tile >> 3) & 3, (tile >> 2) & 1, tile & 3]
                weight = mask_s[g, s].astype(F32) * coup_s[g, s]
                carried.append((weight * dot(inter[g, s], picked)).astype(BF))
            sum_ref[g] += lax.dot_general(
                jnp.concatenate(carried, axis=1),
                jnp.concatenate([inter[g, s] for s in range(8)], axis=1),
                (((1,), (1,)), ((), ())), preferred_element_type=F32,
            )

    for name in started:
        cp[name].wait_send()


def shards(
    half_ints, pno_coef, pair_list, fit_domain, fit_factor, amplitudes, pno_energy, occ_energy,
    partners, partner_mask, intersections, coupling,
):
    any_spec = pl.BlockSpec(memory_space=pl.ANY)
    vmem_spec = pl.BlockSpec(memory_space=pltpu.VMEM)
    total, denominator = pl.pallas_call(
        kernel,
        out_shape=(
            pltpu.VMEM((4, 128, 128), F32),
            pltpu.VMEM((4, 128, 128), F32),
        ),
        in_specs=[any_spec] * 12,
        out_specs=(vmem_spec, vmem_spec),
        scratch_shapes=[
            pltpu.VMEM((2, 4096, 256), BF),
            pltpu.VMEM((2, 256, 4096), BF),
        ]
        + [pltpu.VMEM((4, 4096, 128), BF)] * 4
        + [
            pltpu.VMEM((4, 4, 2, 4, 128, 128), BF),
            pltpu.VMEM((1024, 128), BF),
            pltpu.VMEM((128, 1024), BF),
            pltpu.VMEM((2, 4, 256, 256), BF),
            pltpu.VMEM((4, 2, 256), jnp.int32),
            pltpu.VMEM((4, 2, 64, 256), BF),
            pltpu.VMEM((3, 2, 64, 256), BF),
            pltpu.VMEM((2, 256, 256), BF),
            pltpu.VMEM((3, 4, 256, 128), BF),
            pltpu.VMEM((2, 2, 256, 128), BF),
            pltpu.VMEM((2, 4, 256, 128), BF),
            pltpu.VMEM((4, 256, 128), F32),
            pltpu.VMEM((4, 8, 128, 128), BF),
            pltpu.VMEM((4, 128), F32),
            pltpu.SMEM((4, 2, 4), jnp.int32),
            pltpu.SMEM((64,), F32),
            pltpu.SMEM((4, 8), jnp.int32),
            pltpu.SMEM((4, 8), jnp.int32),
            pltpu.SMEM((4, 8), F32),
            pltpu.SemaphoreType.DMA((COPIES,)),
            pltpu.SemaphoreType.DMA((COPIES,)),
            pltpu.SemaphoreType.DMA((8,)),
            pltpu.SemaphoreType.DMA((4,)),
            pltpu.SemaphoreType.DMA((10,)),
        ],
        compiler_params=pltpu.CompilerParams(
            collective_id=0, has_side_effects=True, vmem_limit_bytes=VMEM_LIMIT
        ),
    )(
        half_ints, pno_coef, jnp.swapaxes(pair_list, 1, 2), fit_domain, fit_factor, amplitudes,
        pno_energy, occ_energy, partners, partner_mask, intersections, coupling,
    )
    amps = amplitudes.astype(F32)
    residual = total + denominator * amps
    return residual, (amps - residual / denominator).astype(BF)


def solution(mesh):
    return jax.shard_map(
        shards,
        mesh=mesh,
        in_specs=(
            P("pair", "basis", None),
            P(None, "pair", "basis", None),
            P(None, "pair", None),
            P("pair", None),
            P("pair", None),
            P(("basis", "pair"), None, None),
            P(("basis", "pair"), None),
            P(),
            P(("basis", "pair"), None),
            P(("basis", "pair"), None),
            P(("basis", "pair"), None, None, None),
            P(("basis", "pair"), None),
        ),
        out_specs=(P(("basis", "pair"), None, None), P(("basis", "pair"), None, None)),
        check_vma=False,
    )
```

```python
import jax
import jax.numpy as jnp
from jax import lax
from jax.experimental import pallas as pl
from jax.experimental.pallas import tpu as pltpu
from jax.sharding import PartitionSpec as P

BF = jnp.bfloat16
F32 = jnp.float32
MESH = pl.DeviceIdType.MESH
COPIES = 73
VMEM_LIMIT = 60 * 1024 * 1024


class N:
    (
        t1p0, t1m1, b1p, b1m, ip, im, i2, t1p1, t1m0, a1p,
        a1m, tf0, g2m, trp, trm, b1rp, b1rm, g2p, gma, tf1,
        tf2, gpa, a1rp, a1rm, b2p0, b2m1, b2p1, b2m0, fb1, tf3,
        fa1, gmb, gpb, fa2m, fa2p, fb2m, fb2p, fa20, fa21,
    ) = range(39)
    a2p, a2m, a2rp, a2rm = range(39, 55, 4)
    rp, rm, r2, zp, zm, z2, b2rp, b2rm, fb2 = range(55, 73, 2)


def kernel(
    half_hbm, coef_hbm, list_hbm, dom_hbm, fit_hbm, amp_hbm, pen_hbm, occ_hbm,
    part_hbm, mask_hbm, inter_hbm, coup_hbm,
    sum_ref, den_ref,
    hbuf, ht, cb0, cb1, cb2, cb3,
    am, fb, ft, tb, fd, rb, rr, dt, pb, gr2, gr, own, inter, pen,
    list_s, occ_s, part_s, mask_s, coup_s,
    send_sem, recv_sem, h_sem, c_sem, in_sem,
):
    cbs = (cb0, cb1, cb2, cb3)
    z = lax.axis_index("basis")
    pair = lax.axis_index("pair")
    x, y, c = pair // 8, (pair // 2) % 4, pair % 2
    xp, xm, x2 = (x + 1) % 4, (x + 3) % 4, (x + 2) % 4
    yp, ym, y2 = (y + 1) % 4, (y + 3) % 4, (y + 2) % 4
    zp, zm, z2 = (z + 1) % 4, (z + 3) % 4, (z + 2) % 4

    def dev(zz, xx, yy, cc):
        return (zz, (xx * 4 + yy) * 2 + cc)

    to = {
        "xp": dev(z, xp, y, c), "xm": dev(z, xm, y, c),
        "yp": dev(z, x, yp, c), "ym": dev(z, x, ym, c), "y2": dev(z, x, y2, c),
        "zp": dev(zp, x, y, c), "zm": dev(zm, x, y, c), "z2": dev(z2, x, y, c),
        "o": dev(z, x, y, 1 - c),
    }
    started = []

    def rdma(name, src, dst, where):
        return pltpu.make_async_remote_copy(
            src_ref=src, dst_ref=dst, send_sem=send_sem.at[name], recv_sem=recv_sem.at[name],
            device_id=to[where], device_id_type=MESH,
        )

    def same(name, ref, where):
        return rdma(name, ref, ref, where)

    every = pl.ds(0, 4)
    cp = {
        N.a1p: same(N.a1p, am.at[x, y, c, pl.ds(0, 2)], "xp"),
        N.a1m: same(N.a1m, am.at[x, y, c, pl.ds(0, 2)], "xm"),
        N.a1rp: same(N.a1rp, am.at[xm, y, c, 0], "xp"),
        N.a1rm: same(N.a1rm, am.at[xp, y, c, 1], "xm"),
        N.b1p: same(N.b1p, am.at[x, y, c, pl.ds(2, 2)], "yp"),
        N.b1m: same(N.b1m, am.at[x, y, c, pl.ds(2, 2)], "ym"),
        N.b1rp: same(N.b1rp, am.at[x, ym, c, 2], "yp"),
        N.b1rm: same(N.b1rm, am.at[x, yp, c, 3], "ym"),
        N.b2p0: same(N.b2p0, am.at[x, every, c, 2], "xp"),
        N.b2p1: same(N.b2p1, am.at[x, every, c, 3], "xp"),
        N.b2m0: same(N.b2m0, am.at[x, every, c, 2], "xm"),
        N.b2m1: same(N.b2m1, am.at[x, every, c, 3], "xm"),
        N.fa1: same(N.fa1, am.at[every, y, c, pl.ds(0, 2)], "o"),
        N.fb1: same(N.fb1, am.at[x, every, c, pl.ds(2, 2)], "o"),
        N.fa2m: same(N.fa2m, am.at[every, ym, c, pl.ds(0, 2)], "o"),
        N.fa2p: same(N.fa2p, am.at[every, yp, c, pl.ds(0, 2)], "o"),
        N.fa20: same(N.fa20, am.at[every, y2, c, 0], "o"),
        N.fa21: same(N.fa21, am.at[every, y2, c, 1], "o"),
        N.fb2m: same(N.fb2m, am.at[xm, every, c, pl.ds(2, 2)], "o"),
        N.fb2p: same(N.fb2p, am.at[xp, every, c, pl.ds(2, 2)], "o"),
        N.t1p0: rdma(N.t1p0, tb.at[0, 0, pl.ds(0, 128)], tb.at[0, 1, pl.ds(0, 128)], "xp"),
        N.t1p1: rdma(N.t1p1, tb.at[0, 0, pl.ds(128, 128)], tb.at[0, 1, pl.ds(128, 128)], "xp"),
        N.t1m0: rdma(N.t1m0, tb.at[0, 0, pl.ds(0, 128)], tb.at[0, 2, pl.ds(0, 128)], "xm"),
        N.t1m1: rdma(N.t1m1, tb.at[0, 0, pl.ds(128, 128)], tb.at[0, 2, pl.ds(128, 128)], "xm"),
        N.trp: rdma(N.trp, tb.at[0, 1, pl.ds(0, 128)], tb.at[0, 3, pl.ds(0, 128)], "xp"),
        N.trm: rdma(N.trm, tb.at[0, 2, pl.ds(128, 128)], tb.at[0, 3, pl.ds(128, 128)], "xm"),
        N.tf0: rdma(N.tf0, tb.at[0, 0], tb.at[1, 0], "o"),
        N.tf1: rdma(N.tf1, tb.at[0, 1], tb.at[1, 1], "o"),
        N.tf2: rdma(N.tf2, tb.at[0, 2], tb.at[1, 2], "o"),
        N.tf3: rdma(N.tf3, tb.at[0, 3], tb.at[1, 3], "o"),
        N.ip: rdma(N.ip, fd.at[0], fd.at[1], "yp"),
        N.im: rdma(N.im, fd.at[0], fd.at[2], "ym"),
        N.i2: rdma(N.i2, fd.at[0], fd.at[3], "y2"),
        N.g2p: rdma(N.g2p, pb.at[0, pl.ds(0, 2)], gr2.at[0], "zp"),
        N.g2m: rdma(N.g2m, pb.at[0, pl.ds(2, 2)], gr2.at[1], "zm"),
        N.gpa: rdma(N.gpa, pb.at[1, pl.ds(2, 2)], gr.at[0, pl.ds(2, 2)], "zp"),
        N.gpb: rdma(N.gpb, pb.at[1, pl.ds(0, 2)], gr.at[0, pl.ds(0, 2)], "zp"),
        N.gma: rdma(N.gma, pb.at[2, pl.ds(0, 2)], gr.at[1, pl.ds(0, 2)], "zm"),
        N.gmb: rdma(N.gmb, pb.at[2, pl.ds(2, 2)], gr.at[1, pl.ds(2, 2)], "zm"),
    }

    for j, row in enumerate((x, xm, xp, x2)):
        cp[N.a2p + j] = same(N.a2p + j, am.at[row, y, c, pl.ds(0, 2)], "yp")
        cp[N.a2m + j] = same(N.a2m + j, am.at[row, y, c, pl.ds(0, 2)], "ym")
        cp[N.a2rp + j] = same(N.a2rp + j, am.at[row, ym, c, 0], "yp")
        cp[N.a2rm + j] = same(N.a2rm + j, am.at[row, yp, c, 1], "ym")

    mine = pl.ds(0, 64)
    for o in range(2):
        lines = pl.ds(2 * o, 2)
        cp[N.b2rp + o] = same(N.b2rp + o, am.at[xm, lines, c, 2], "xp")
        cp[N.b2rm + o] = same(N.b2rm + o, am.at[xp, lines, c, 3], "xm")
        cp[N.fb2 + o] = same(N.fb2 + o, am.at[x2, lines, c, pl.ds(2, 2)], "o")
        cp[N.rp + o] = rdma(N.rp + o, rb.at[2, o], rr.at[0, o], "yp")
        cp[N.rm + o] = rdma(N.rm + o, rb.at[1, o], rr.at[1, o], "ym")
        cp[N.r2 + o] = rdma(N.r2 + o, rb.at[3, o], rr.at[2, o], "y2")
        cp[N.zp + o] = rdma(N.zp + o, dt.at[o, mine], dt.at[o, pl.ds(64, 64)], "zp")
        cp[N.zm + o] = rdma(N.zm + o, dt.at[o, mine], dt.at[o, pl.ds(128, 64)], "zm")
        cp[N.z2 + o] = rdma(N.z2 + o, dt.at[o, mine], dt.at[o, pl.ds(192, 64)], "z2")

    def go(*names):
        for name in names:
            cp[name].start()
            started.append(name)

    def got(*names):
        for name in names:
            cp[name].wait_recv()

    lane = pl.multiple_of((z // 2) * 128, 128)
    small = [
        pltpu.make_async_copy(amp_hbm, am.at[x, y, c], in_sem.at[0]),
        pltpu.make_async_copy(dom_hbm, fd.at[0], in_sem.at[1]),
        pltpu.make_async_copy(fit_hbm.at[:, pl.ds(lane, 128)], fb, in_sem.at[2]),
        pltpu.make_async_copy(list_hbm, list_s, in_sem.at[3]),
        pltpu.make_async_copy(occ_hbm, occ_s, in_sem.at[4]),
        pltpu.make_async_copy(part_hbm, part_s, in_sem.at[5]),
        pltpu.make_async_copy(mask_hbm, mask_s, in_sem.at[6]),
        pltpu.make_async_copy(coup_hbm, coup_s, in_sem.at[7]),
        pltpu.make_async_copy(pen_hbm, pen, in_sem.at[8]),
    ]
    blocks = [z2, zp, zm, z]

    def h_copy(k, o):
        rows = pl.ds(k * 1024, 1024)
        return pltpu.make_async_copy(half_hbm.at[o, rows], hbuf.at[o, rows], h_sem.at[k * 2 + o])

    def c_copy(k):
        return pltpu.make_async_copy(coef_hbm.at[blocks[k]], cbs[k], c_sem.at[k])

    barrier = pltpu.get_barrier_semaphore()
    for place in to.values():
        pl.semaphore_signal(barrier, inc=1, device_id=place, device_id_type=MESH)
    for i in (2, 0, 1, 3, 4, 5, 6, 7, 8):
        small[i].start()
    h_copies = [(h_copy(k, 0), h_copy(k, 1)) for k in range(4)]
    for both in h_copies:
        both[0].start()
        both[1].start()
    c_copies = [c_copy(k) for k in range(4)]
    c_copies[0].start()
    inter_copy = pltpu.make_async_copy(inter_hbm, inter, in_sem.at[9])

    small[2].wait()
    ft[...] = fb[...].T
    side = pl.multiple_of((z % 2) * 64, 64)
    for h in range(4):
        tb[0, 0, h * 64:(h + 1) * 64, :] = ft[pl.ds(side, 64), h * 256:(h + 1) * 256]
    small[0].wait()
    small[1].wait()
    pl.semaphore_wait(barrier, len(to))
    go(N.t1p0, N.t1m1, N.b1p, N.b1m, N.ip, N.im, N.i2, N.t1p1, N.t1m0, N.a1p, N.a1m, N.a2p + 0, N.a2m + 0, N.tf0)
    small[3].wait()

    def arrange(block):
        label = [list_s[block, 0, p] & 1 for p in range(4)]
        common = jnp.where(label[0] + label[1] + label[2] + label[3] >= 2, 1, 0)
        like = [1 - (one ^ common) for one in label]
        many = like[0] + like[1] + like[2] + like[3]
        seen = 0
        place = []
        for p in range(4):
            place.append(jnp.where(like[p] == 1, seen, many + p - seen))
            seen = seen + like[p]
        pick = [sum(jnp.where(place[p] == j, p, 0) for p in range(1, 4)) for j in range(4)]
        third = jnp.where(many >= 3, common, 1 - common)
        fourth = jnp.where(many == 4, common, 1 - common)
        return common, pick, third, fourth, place

    plans = [arrange(block) for block in blocks]

    def turn(k):
        for o in range(2):
            for i in range(4):
                part = slice(k * 1024 + i * 256, k * 1024 + (i + 1) * 256)
                ht[o, :, part] = hbuf[o, part, :].T

    def wide(block, i, j):
        pick = plans[block][1]
        return jnp.concatenate([cbs[block][pick[i]], cbs[block][pick[j]]], axis=1)

    def dot(a, b):
        return jnp.dot(a, b, preferred_element_type=F32)

    def halves(out):
        return out[:, :128], out[:, 128:]

    def even(block, other):
        first = dot(ht[plans[block][0]], wide(block, 0, 1))
        second = dot(ht[plans[other][0]], wide(other, 0, 1))
        return halves(first), halves(second)

    def mixed(block):
        weights = wide(block, 2, 3)
        zero = dot(ht[0], weights)
        one = dot(ht[1], weights)
        third, fourth = plans[block][2], plans[block][3]
        return (
            jnp.where(third == 1, one[:, :128], zero[:, :128]),
            jnp.where(fourth == 1, one[:, 128:], zero[:, 128:]),
        )

    def keep(slot, at, pair_of, arrived=None):
        for i in range(2):
            value = pair_of[i]
            if arrived is not None:
                value = value + gr2[arrived, i].astype(F32)
            pb[slot, at + i] = value.astype(BF)

    for k in range(4):
        h_copies[k][0].wait()
        h_copies[k][1].wait()
        turn(k)
        if k == 1:
            c_copies[2].start()
    c_copies[0].wait()
    c_copies[1].start()
    keep(0, 2, mixed(0))
    go(N.g2m)
    got(N.t1p0)
    go(N.trp)
    got(N.t1m1)
    go(N.trm)
    got(N.b1p)
    go(N.b1rp)
    got(N.b1m)
    go(N.b1rm)
    c_copies[2].wait()
    c_copies[3].start()
    inter_copy.start()
    first, second = even(0, 2)
    keep(0, 0, first)
    go(N.g2p)
    keep(2, 0, second)
    go(N.gma)
    got(N.a2p + 0)
    go(N.a2rp + 0)
    got(N.a2m + 0)
    go(N.a2rm + 0)
    got(N.t1p1)
    go(N.tf1)
    got(N.t1m0)
    go(N.tf2)
    c_copies[1].wait()
    keep(1, 2, mixed(1))
    go(N.gpa)
    got(N.a1p)
    go(N.a1rp, N.a2p + 1, N.a2m + 1)
    got(N.a1m)
    go(N.a1rm, N.a2p + 2, N.a2m + 2)
    got(N.b1rp, N.b1rm)
    go(N.b2p0, N.b2m1, N.b2p1, N.b2m0, N.fb1)
    got(N.trp, N.trm)
    go(N.tf3)
    c_copies[3].wait()
    first, second = even(1, 3)
    own[0], own[1] = second
    third = mixed(2)
    got(N.a1rp, N.a1rm)
    go(N.a2p + 3, N.a2m + 3, N.fa1)
    got(N.g2m)
    keep(2, 2, third, 1)
    go(N.gmb)
    got(N.g2p)
    keep(1, 0, first, 0)
    go(N.gpb)

    got(N.tf0, N.tf1, N.tf2, N.tf3, N.ip, N.im, N.i2)
    iota = lax.broadcasted_iota(jnp.int32, (256, 256), 0)
    sources = [
        (k, j, (xx * 4 + y) * 2 + cc)
        for k, cc in ((0, c), (1, 1 - c))
        for j, xx in enumerate((x, xm, xp, x2))
    ]

    def select(*wanted_of):
        parts = []
        for j, o in wanted_of:
            wanted = fd[j, o:o + 1, :]
            parts.append((wanted >> 10, wanted & 255, (wanted >> 8) & 3))
        totals = [jnp.zeros((256, 256), F32) for _ in parts]
        for k, i, source in sources:
            for n, (owner, row, _) in enumerate(parts):
                key = jnp.where(owner == source, row, -1)
                hot = jnp.where(iota == key, 1.0, 0.0).astype(BF)
                totals[n] = totals[n] + dot(tb[k, i], hot)
        for n, (j, o) in enumerate(wanted_of):
            out = jnp.zeros((64, 256), F32)
            for h in range(4):
                out = out + jnp.where(parts[n][2] == h, totals[n][h * 64:(h + 1) * 64], 0.0)
            rb[j, o] = out.astype(BF)

    def rows(o):
        got(N.rp + o, N.rm + o, N.r2 + o)
        dt[o, 0:64, :] = (
            (rb[0, o].astype(F32) + rr[0, o].astype(F32)) + (rr[1, o].astype(F32) + rr[2, o].astype(F32))
        ).astype(BF)
        go(N.z2 + o, N.zp + o, N.zm + o)

    select((3, 0), (2, 0))
    go(N.r2 + 0, N.rp + 0)
    select((1, 0), (3, 1))
    go(N.rm + 0, N.r2 + 1)
    got(N.b2p0)
    go(N.b2rp + 0, N.b2rp + 1)
    got(N.b2m1)
    go(N.b2rm + 0, N.b2rm + 1)
    select((2, 1), (1, 1))
    go(N.rp + 1, N.rm + 1)
    for j in (1, 2):
        got(N.a2p + j)
        go(N.a2rp + j)
        got(N.a2m + j)
        go(N.a2rm + j)
    select((0, 0), (0, 1))
    got(N.a2p + 3)
    go(N.a2rp + 3, N.fa2m)
    got(N.a2m + 3)
    go(N.a2rm + 3, N.fa2p)
    own[2], own[3] = mixed(3)
    got(N.b2p1)
    go(N.fb2m)
    got(N.b2m0)
    go(N.fb2p)
    rows(0)
    rows(1)
    for i in (4, 5, 6, 7, 8):
        small[i].wait()
    for g in range(4):
        occ = occ_s[list_s[z, 0, g]] + occ_s[list_s[z, 1, g]]
        across = jnp.broadcast_to(pen[g:g + 1, :], (128, 128))
        den_ref[g] = (across.T + across) - occ
    for o in range(2):
        got(N.b2rp + o, N.b2rm + o)
        go(N.fb2 + o)
    got(N.a2rp + 0, N.a2rp + 1, N.a2rp + 2, N.a2rp + 3)
    go(N.fa20)
    got(N.a2rm + 0, N.a2rm + 1, N.a2rm + 2, N.a2rm + 3)
    go(N.fa21)

    got(N.gpa, N.gpb, N.gma, N.gmb)
    place = plans[3][4]
    factors = [
        (own[place[g]] + gr[0, place[g]].astype(F32) + gr[1, place[g]].astype(F32)).astype(BF) for g in range(4)
    ]
    inter_copy.wait()

    @pl.when(c == 0)
    def _():
        got(N.fa1, N.fb1, N.fa2m, N.fa2p, N.fa20, N.fa21, N.fb2m, N.fb2p, N.fb2 + 0, N.fb2 + 1)
        for g in range(4):
            carried = []
            for s in range(8):
                tile = part_s[g, s] & 127
                picked = am[tile >> 5, (tile >> 3) & 3, (tile >> 2) & 1, tile & 3]
                weight = mask_s[g, s].astype(F32) * coup_s[g, s]
                carried.append((weight * dot(inter[g, s], picked)).astype(BF))
            sum_ref[g] = lax.dot_general(
                jnp.concatenate(carried, axis=1),
                jnp.concatenate([inter[g, s] for s in range(8)], axis=1),
                (((1,), (1,)), ((), ())), preferred_element_type=F32,
            )

        got(N.zp + 0, N.zm + 0, N.z2 + 0, N.zp + 1, N.zm + 1, N.z2 + 1)
        fits = [dot(dt[list_s[z, 0, g] & 1], factors[g]).astype(BF) for g in range(4)]
        for g in range(4):
            exchange = lax.dot_general(fits[g], fits[g], (((0,), (0,)), ((), ())), preferred_element_type=F32)
            sum_ref[g] += exchange / 256

    @pl.when(c == 1)
    def _():
        got(N.zp + 0, N.zm + 0, N.z2 + 0, N.zp + 1, N.zm + 1, N.z2 + 1)
        fits = [dot(dt[list_s[z, 0, g] & 1], factors[g]).astype(BF) for g in range(4)]
        for g in range(4):
            exchange = lax.dot_general(fits[g], fits[g], (((0,), (0,)), ((), ())), preferred_element_type=F32)
            sum_ref[g] = exchange / 256
        got(N.fa1, N.fb1, N.fa2m, N.fa2p, N.fa20, N.fa21, N.fb2m, N.fb2p, N.fb2 + 0, N.fb2 + 1)
        for g in range(4):
            carried = []
            for s in range(8):
                tile = part_s[g, s] & 127
                picked = am[tile >> 5, (tile >> 3) & 3, (tile >> 2) & 1, tile & 3]
                weight = mask_s[g, s].astype(F32) * coup_s[g, s]
                carried.append((weight * dot(inter[g, s], picked)).astype(BF))
            sum_ref[g] += lax.dot_general(
                jnp.concatenate(carried, axis=1),
                jnp.concatenate([inter[g, s] for s in range(8)], axis=1),
                (((1,), (1,)), ((), ())), preferred_element_type=F32,
            )

    for name in started:
        cp[name].wait_send()


def shards(
    half_ints, pno_coef, pair_list, fit_domain, fit_factor, amplitudes, pno_energy, occ_energy,
    partners, partner_mask, intersections, coupling,
):
    any_spec = pl.BlockSpec(memory_space=pl.ANY)
    vmem_spec = pl.BlockSpec(memory_space=pltpu.VMEM)
    total, denominator = pl.pallas_call(
        kernel,
        out_shape=(
            pltpu.VMEM((4, 128, 128), F32),
            pltpu.VMEM((4, 128, 128), F32),
        ),
        in_specs=[any_spec] * 12,
        out_specs=(vmem_spec, vmem_spec),
        scratch_shapes=[
            pltpu.VMEM((2, 4096, 256), BF),
            pltpu.VMEM((2, 256, 4096), BF),
        ]
        + [pltpu.VMEM((4, 4096, 128), BF)] * 4
        + [
            pltpu.VMEM((4, 4, 2, 4, 128, 128), BF),
            pltpu.VMEM((1024, 128), BF),
            pltpu.VMEM((128, 1024), BF),
            pltpu.VMEM((2, 4, 256, 256), BF),
            pltpu.VMEM((4, 2, 256), jnp.int32),
            pltpu.VMEM((4, 2, 64, 256), BF),
            pltpu.VMEM((3, 2, 64, 256), BF),
            pltpu.VMEM((2, 256, 256), BF),
            pltpu.VMEM((3, 4, 256, 128), BF),
            pltpu.VMEM((2, 2, 256, 128), BF),
            pltpu.VMEM((2, 4, 256, 128), BF),
            pltpu.VMEM((4, 256, 128), F32),
            pltpu.VMEM((4, 8, 128, 128), BF),
            pltpu.VMEM((4, 128), F32),
            pltpu.SMEM((4, 2, 4), jnp.int32),
            pltpu.SMEM((64,), F32),
            pltpu.SMEM((4, 8), jnp.int32),
            pltpu.SMEM((4, 8), jnp.int32),
            pltpu.SMEM((4, 8), F32),
            pltpu.SemaphoreType.DMA((COPIES,)),
            pltpu.SemaphoreType.DMA((COPIES,)),
            pltpu.SemaphoreType.DMA((8,)),
            pltpu.SemaphoreType.DMA((4,)),
            pltpu.SemaphoreType.DMA((10,)),
        ],
        compiler_params=pltpu.CompilerParams(
            collective_id=0, has_side_effects=True, vmem_limit_bytes=VMEM_LIMIT
        ),
    )(
        half_ints, pno_coef, jnp.swapaxes(pair_list, 1, 2), fit_domain, fit_factor, amplitudes,
        pno_energy, occ_energy, partners, partner_mask, intersections, coupling,
    )
    amps = amplitudes.astype(F32)
    residual = total + denominator * amps
    return residual, (amps - residual / denominator).astype(BF)


def solution(mesh):
    return jax.shard_map(
        shards,
        mesh=mesh,
        in_specs=(
            P("pair", "basis", None),
            P(None, "pair", "basis", None),
            P(None, "pair", None),
            P("pair", None),
            P("pair", None),
            P(("basis", "pair"), None, None),
            P(("basis", "pair"), None),
            P(),
            P(("basis", "pair"), None),
            P(("basis", "pair"), None),
            P(("basis", "pair"), None, None, None),
            P(("basis", "pair"), None),
        ),
        out_specs=(P(("basis", "pair"), None, None), P(("basis", "pair"), None, None)),
        check_vma=False,
    )
```
